32 devices in a mesh: beam: 1, freq: 32 (over z, y, x, core), tm: 1.
Axes of the slice: x: 2, y: 2, z: 4, core: 2. Of those that a mesh axis runs over, the one named last changes fastest.
Arguments:
- data: bfloat16 [4096, 640], P(('beam', 'freq'), 'tm'), may hold values from -1000 to 1000
- chan_delay: int32 [64, 4096], P(None, 'freq'), may hold values from 0 to 40, as said below
- sub_delay: int32 [2048, 64], P('freq'), may hold values from 0 to 24, as said below
- widths: int32 [16], replicated, may hold values from 1 to 256, as said below
Outputs:
- snr: float32 [2048, 16], P(('beam', 'freq'))
The draws below stay inside these ranges and needn't reach their ends.
Inputs may be any that keep to these rules, and one draw needn't show every extreme that they name: chan_delay[s, c] is never smaller for a larger trial s; the value 40 is reached. sub_delay[d, b] is never smaller for a larger trial d; the value 24 is reached. The widths are distinct and include 1 and 256.
All inputs are finite; a program needn't handle non-finite values.
Results may differ from the reference program's by a relative error of at most 0.0014.
Values may be sent and summed in bfloat16 or wider, within the bound.
A program may use at most 64 MiB of HBM per device.

```python
import math
import jax
import jax.numpy as jnp
from jax import lax

NCHAN = 4096
NSUB = 64
NSDM = 64
NDM = 2048
WMAX = 256
NW = 16
CPS = 64
DPS = 32
D1MAX = 40
D2MAX = 24
NT = 640


def draw_data(key, part):
    k_noise, k_gain, k_base = jax.random.split(key, 3)
    gain = jnp.exp(jax.random.uniform(k_gain, (NCHAN, 1), jnp.float32, 0.0, math.log(10.0)))
    times = jnp.arange(NT, dtype=jnp.float32)[None, :] / NT
    noise = jnp.clip(jax.random.normal(k_noise, (NCHAN, NT), jnp.float32), -5.0, 5.0)
    envelope = 3.0 ** times
    baseline = 0.5 * jnp.clip(jax.random.normal(k_base, (NCHAN, 1), jnp.float32), -3.0, 3.0)
    return (gain * (envelope * noise + baseline)).astype(jnp.bfloat16)


def draw_chan_delay(key, part):
    k_steps, k_top = jax.random.split(key, 2)
    increments = jax.random.randint(k_steps, (NSUB, CPS), 1, 5)
    column = jnp.arange(CPS, dtype=jnp.int32)[None, :]
    increments = jnp.where(column == 0, 0, increments)
    curve = jnp.cumsum(increments, axis=1)
    tops = jax.random.randint(k_top, (NSUB,), D1MAX // 2, D1MAX + 1)
    band = jnp.arange(NSUB, dtype=jnp.int32)
    tops = jnp.where(band == 0, D1MAX, tops).astype(jnp.int32)
    trial = jnp.arange(1, NSDM + 1, dtype=jnp.int32)
    delay = trial[:, None, None] * curve[None, :, :] * tops[None, :, None] // (NSDM * curve[None, :, CPS - 1:CPS])
    return delay.reshape(NSDM, NCHAN).astype(jnp.int32)


def draw_sub_delay(key, part):
    increments = jax.random.randint(key, (NSUB,), 1, 5)
    column = jnp.arange(NSUB, dtype=jnp.int32)
    increments = jnp.where(column == 0, 0, increments)
    curve = jnp.cumsum(increments)
    trial = jnp.arange(1, NDM + 1, dtype=jnp.int32)
    delay = trial[:, None] * curve[None, :] * D2MAX // (NDM * curve[NSUB - 1])
    return delay.astype(jnp.int32)


def draw_widths(key, part):
    chosen = jax.random.permutation(key, WMAX - 2)[:NW - 2] + 2
    first = jnp.ones((1,), jnp.int32)
    last = jnp.full((1,), WMAX, jnp.int32)
    return jnp.concatenate([first, chosen.astype(jnp.int32), last]).astype(jnp.int32)


def setup_inputs(seed: int = 0, part: int = 0) -> dict:
    arg_keys = jax.random.split(jax.random.key(seed), 5)
    part_keys = jax.random.split(jax.random.fold_in(arg_keys[4], part), 5)
    return {
        "data": draw_data(jax.random.fold_in(jax.random.fold_in(arg_keys[4], part), 71), part),
        "chan_delay": draw_chan_delay(jax.random.fold_in(arg_keys[4], 71), part),
        "sub_delay": draw_sub_delay(jax.random.fold_in(arg_keys[4], 71), part),
        "widths": draw_widths(jax.random.fold_in(arg_keys[4], 71), part),
    }


def subband_sum(slab, delays, length):

    def one_trial(row_delays):
        return jax.vmap(lambda channel_row, offset: lax.dynamic_slice_in_dim(channel_row, offset, length))(slab, row_delays)
    picked = jax.vmap(one_trial)(delays)
    return lax.optimization_barrier(jnp.sum(picked, axis=1, dtype=jnp.float32)).astype(jnp.bfloat16)

def dedisperse(series, delays, length):

    def one_trial(row_delays):
        return jax.vmap(lambda band_row, offset: lax.dynamic_slice_in_dim(band_row, offset, length))(series, row_delays)
    picked = jax.vmap(one_trial)(delays)
    return lax.optimization_barrier(jnp.sum(picked, axis=1, dtype=jnp.float32))

def peak_scores(normed, widths, span):
    running = jnp.concatenate([jnp.zeros((normed.shape[0], 1), normed.dtype), jnp.cumsum(normed, axis=1)], axis=1)

    def one_width(width):
        upper = lax.dynamic_slice_in_dim(running, width, span, 1)
        return lax.optimization_barrier(jnp.max((upper - running[:, :span]) / jnp.sqrt(width.astype(jnp.float32)), axis=1))
    return lax.map(one_width, widths).T

def reference(data, chan_delay, sub_delay, widths):
    tail_span = D1MAX + D2MAX + WMAX
    extended = jnp.concatenate([data, jnp.zeros((NCHAN, tail_span), jnp.bfloat16)], axis=1)
    sub_len = NT + D2MAX + WMAX
    channel_slabs = extended.reshape(NSUB, CPS, extended.shape[1])
    trial_delays = chan_delay.reshape(NSDM, NSUB, CPS).transpose(1, 0, 2)
    subband = lax.map(lambda members: subband_sum(members[0], members[1], sub_len), (channel_slabs, trial_delays))
    dm_len = NT + WMAX
    grouped = sub_delay.reshape(NSDM, DPS, NSUB)
    series = lax.map(lambda members: dedisperse(members[0], members[1], dm_len), (jnp.moveaxis(subband, 1, 0), grouped))
    series = series.reshape(NDM, dm_len)
    inside = series[:, :NT]
    average = lax.optimization_barrier(jnp.mean(inside, axis=1))
    deviation = jnp.sqrt(lax.optimization_barrier(jnp.mean((inside - average[:, None]) ** 2, axis=1)) + 1e-05)
    normed = (series - average[:, None]) / deviation[:, None]
    return peak_scores(normed, widths, NT)
```

```python
import functools

import jax
import jax.numpy as jnp
from jax import lax
from jax.experimental import pallas as pl
from jax.experimental.pallas import tpu as pltpu
from jax.sharding import PartitionSpec as P

NSUB = 64
NSDM = 64
WMAX = 256
CPS = 64
DPS = 32
D1MAX = 40
D2MAX = 24


def passed_along(value, axis, steps):
    count = lax.axis_size(axis)
    initial, last = (max(0, -steps), min(count, count - steps))
    return lax.ppermute(value, axis, [(source, source + steps) for source in range(initial, last)])


def shifted_sum(source, delays, length, largest):
    band_count = source.shape[0]
    trial_count = delays.shape[1]
    start_total = jnp.zeros((band_count, trial_count, length), jnp.float32)

    def add_shifts(step_index, running_total):
        for within in range(2):
            offset = 2 * step_index + within
            window = lax.dynamic_slice_in_dim(source, offset, length, 2)
            selector = (delays == offset).astype(jnp.bfloat16)
            running_total = running_total + jnp.einsum(
                "bsm,bmt->bst", selector, window, preferred_element_type=jnp.float32
            )
        return running_total

    return lax.fori_loop(0, (largest + 2) // 2, add_shifts, start_total)


def form_subbands(extended, chan_delay, length):
    band_count = extended.shape[0] // CPS
    channel_slabs = extended.reshape(band_count, CPS, extended.shape[1])
    trial_delays = chan_delay.reshape(NSDM, band_count, CPS).transpose(1, 0, 2)
    return shifted_sum(channel_slabs, trial_delays, length, D1MAX).astype(jnp.bfloat16)


def prefix_sums(values):
    step = 1
    while step < values.shape[1]:
        values = values + jnp.pad(values[:, :-step], ((0, 0), (step, 0)))
        step *= 2
    return values


def peak_scores(normed, widths, span):
    running = jnp.concatenate([jnp.zeros((normed.shape[0], 1), normed.dtype), prefix_sums(normed)], axis=1)

    def one_width(width):
        upper = lax.dynamic_slice_in_dim(running, width, span, 1)
        return jnp.max((upper - running[:, :span]) / jnp.sqrt(width.astype(jnp.float32)), axis=1)

    return lax.map(one_width, widths).T


def on_device(data, chan_delay, sub_delay, widths):
    block_len = data.shape[1]
    total_len = block_len * lax.axis_size("tm")
    edge_rows = passed_along(data[:, :D1MAX], "tm", -1)
    extended = jnp.concatenate([data, edge_rows], axis=1)
    subband = form_subbands(extended, chan_delay, block_len)
    regrouped = lax.all_to_all(subband, "freq", split_axis=1, concat_axis=0, tiled=True)
    later = passed_along(regrouped[:, :, : D2MAX + WMAX], "tm", -1)
    regrouped = jnp.concatenate([regrouped, later], axis=2)
    dm_len = block_len + WMAX
    local_trials = regrouped.shape[1]
    grouped = sub_delay.reshape(local_trials, DPS, NSUB)
    by_trial = jnp.transpose(regrouped, (1, 0, 2))
    series = shifted_sum(by_trial, grouped, dm_len, D2MAX)
    series = series.reshape(local_trials * DPS, dm_len)
    inside = series[:, :block_len]
    totals = lax.psum(jnp.sum(inside, axis=1), "tm")
    average = totals / total_len
    centred = lax.psum(jnp.sum((inside - average[:, None]) ** 2, axis=1), "tm")
    spread = centred / total_len
    deviation = jnp.sqrt(spread + 1e-05)
    normed = (series - average[:, None]) / deviation[:, None]
    local_peaks = peak_scores(normed, widths, block_len)
    return lax.pmax(local_peaks, "tm")

LOWS = 4


def fused_kernel(peers, block_len, data_hbm, chan_hbm, sub_hbm, width_hbm, out_ref,
                 data_ref, chan_ref, sub_ref, width_ref, load_sem, select, shifted, picks, moved, outgoing, incoming,
                 running, send_sem, recv_sem):
    me = lax.axis_index("freq")
    rows = data_ref.shape[0]
    bands = rows // CPS
    own_trials = NSDM // peers
    dms = sub_ref.shape[0]
    group = bands * own_trials
    f32, bf16 = jnp.float32, jnp.bfloat16
    highs = D1MAX // LOWS + 1
    sub_highs = D2MAX // LOWS + 1
    blocks = block_len // 128

    loads = [
        pltpu.make_async_copy(source, target, load_sem.at[index])
        for index, (source, target) in enumerate((
            (chan_hbm, chan_ref), (data_hbm, data_ref), (sub_hbm, sub_ref), (width_hbm, width_ref)))
    ]
    for load in loads:
        load.start()

    barrier = pltpu.get_barrier_semaphore()

    def greet(step, carry):
        pl.semaphore_signal(barrier, inc=1, device_id={"freq": lax.rem(me + step, peers)},
                            device_id_type=pl.DeviceIdType.MESH)
        return carry

    lax.fori_loop(1, peers, greet, 0)

    def iota(shape, axis):
        return lax.broadcasted_iota(jnp.int32, shape, axis)

    def shift_rows(block, target, first, count):
        wide = block.astype(f32)
        lane = iota(wide.shape, 1)
        for low in range(LOWS):
            piece = wide
            if low:
                piece = jnp.where(lane < block_len - low, pltpu.roll(wide, block_len - low, 1), 0.0)
            target[low * count + first:low * count + first + wide.shape[0], :] = piece.astype(bf16)

    def total_of(product, count, count_highs):
        lane = iota((count, 128), 1)
        sums = [product[0:count, 128 * i:128 * (i + 1)] for i in range(blocks)]
        for high in range(1, count_highs):
            step = LOWS * high
            turned = [
                pltpu.roll(product[high * count:(high + 1) * count, 128 * i:128 * (i + 1)], 128 - step, 1)
                for i in range(blocks)
            ] + [0.0]
            for i in range(blocks):
                sums[i] = sums[i] + jnp.where(lane < 128 - step, turned[i], turned[i + 1])
        return sums

    def pick_trials(first, count):
        lane = iota((count, rows), 1)
        chan = chan_ref[first:first + count, :]
        other = pltpu.roll(chan, CPS, 1)
        for band in range(bands):
            near, far = (chan, other) if band == 0 else (other, chan)
            pair = jnp.where(lane < CPS, near, far - 1)
            for high in range(highs):
                for half in range(LOWS // 2):
                    block = jnp.where(pair == LOWS * high + 2 * half, 1.0, 0.0).astype(bf16)
                    start = highs * first + high * count
                    select[band, start:start + count, 128 * half:128 * (half + 1)] = block

    def form(first, count):
        for band in range(bands):
            start = highs * first
            product = jnp.dot(select[band, start:start + highs * count, :], shifted[band],
                              preferred_element_type=f32)
            sums = total_of(product, count, highs)
            for i in range(blocks):
                outgoing[first // own_trials:(first + count) // own_trials, own_trials * band:own_trials * (band + 1),
                         128 * i:128 * (i + 1)] = sums[i].astype(bf16).reshape(count // own_trials, own_trials, 128)

    quarter = peers // 4

    def sending(target):
        return pltpu.make_async_remote_copy(
            src_ref=outgoing.at[target], dst_ref=incoming.at[me],
            send_sem=send_sem, recv_sem=recv_sem.at[me // quarter],
            device_id={"freq": target}, device_id_type=pl.DeviceIdType.MESH)

    def start_one(target, carry):
        @pl.when(target != me)
        def _():
            sending(target).start()
        return carry

    first_trials = NSDM // 4
    loads[0].wait()
    pick_trials(0, first_trials)
    loads[1].wait()
    for band in range(bands):
        shift_rows(data_ref[band * CPS:(band + 1) * CPS, :], shifted.at[band], 0, CPS)
    form(0, first_trials)
    pl.semaphore_wait(barrier, peers - 1)
    lax.fori_loop(0, quarter, start_one, 0)
    pick_trials(first_trials, NSDM - first_trials)
    form(first_trials, NSDM - first_trials)
    lax.fori_loop(quarter, peers, start_one, 0)
    own = pltpu.make_async_copy(outgoing.at[me], incoming.at[me], recv_sem.at[me // quarter])
    own.start()

    loads[2].wait()
    loads[3].wait()
    trial_dms = dms // own_trials
    half_rows = rows // 2
    sub = sub_ref[...].astype(f32).astype(bf16)
    for half in range(2):
        lane = iota((NSUB, 128), 1)
        row = half * half_rows + lane % half_rows
        spread = (row // own_trials == iota((NSUB, 128), 0)).astype(f32).astype(bf16)
        delay = jnp.dot(sub, spread, preferred_element_type=f32)
        lane = iota((dms, 128), 1)
        delay = delay - (lane // half_rows).astype(f32)
        delay = jnp.where(lane % own_trials == iota((dms, 128), 0) // trial_dms, delay, -99.0)
        for high in range(sub_highs):
            for pair in range(LOWS // 2):
                picks[half, high * dms:(high + 1) * dms, 128 * pair:128 * (pair + 1)] = jnp.where(
                    delay == float(LOWS * high + 2 * pair), 1.0, 0.0).astype(bf16)
    below = (iota((136, 256), 1) % 128 < iota((136, 256), 0)).astype(f32).astype(bf16)

    def arrived(index):
        part = incoming.at[index * quarter:(index + 1) * quarter]
        pltpu.make_async_copy(part, part, recv_sem.at[index]).wait()
        block = jnp.concatenate(
            [incoming[index * quarter:(index + 1) * quarter, :, 128 * i:128 * (i + 1)].reshape(rows // 4, 128)
             for i in range(blocks)], axis=1)
        shift_rows(block, moved.at[index // 2], index % 2 * (rows // 4), half_rows)

    def half_series(half):
        product = jnp.dot(picks[half], moved[half], preferred_element_type=f32)
        return total_of(product, dms, sub_highs)

    arrived(0)
    arrived(1)
    early = half_series(0)
    arrived(2)
    arrived(3)
    late = half_series(1)
    sent = outgoing.at[0:peers - 1]
    pltpu.make_async_copy(sent, sent, send_sem).wait()

    series = [a + b for a, b in zip(early, late)]
    average = jnp.sum(sum(series), axis=1, keepdims=True) / block_len
    centred = [block - average for block in series]
    spread = jnp.sum(sum(block * block for block in centred), axis=1, keepdims=True) / block_len
    deviation = jnp.sqrt(spread + 1e-05)
    across = jnp.broadcast_to(deviation, (dms, 128)).T[0:1, :]
    centred = centred + [jnp.broadcast_to(-average, (dms, 128))] * (WMAX // 128)
    heads = [block.astype(bf16) for block in centred]
    tails = [(block - head.astype(f32)).astype(bf16) for block, head in zip(centred, heads)]
    ahead = blocks + WMAX // 128 - blocks
    carry = jnp.zeros((1, 2 * dms), f32)
    for i in range(blocks):
        j = i + 2
        block = jnp.concatenate([
            jnp.concatenate([heads[i], tails[i]], axis=1), jnp.concatenate([heads[j], tails[j]], axis=1)], axis=0)
        sums = lax.dot_general(below, block, (((1,), (1,)), ((), ())), preferred_element_type=f32)
        running[128 * i:128 * (i + 1), :] = sums[0:128, :] + carry
        carry = carry + sums[128:129, :]

    span = block_len - 256
    base = running[0:span, :]
    peaks = []
    for index in range(width_ref.shape[0]):
        width = width_ref[index]
        upper = running[pl.ds(width, span), :]
        peaks.append(jnp.max(upper - base, axis=0, keepdims=True))
    peaks = jnp.concatenate(peaks, axis=0)
    peaks = jnp.maximum(peaks, pltpu.roll(peaks, dms, 1))
    scales = jnp.concatenate(
        [jnp.full((1, dms), width_ref[index].astype(f32)) for index in range(width_ref.shape[0])], axis=0)
    out_ref[...] = peaks[:, 0:dms] / (across * jnp.sqrt(scales))


def fused(data, chan_delay, sub_delay, widths):
    peers = lax.axis_size("freq")
    rows, block_len = data.shape
    bands = rows // CPS
    dms = sub_delay.shape[0]
    group = bands * (NSDM // peers)
    highs = D1MAX // LOWS + 1
    sub_highs = D2MAX // LOWS + 1
    anywhere = pl.BlockSpec(memory_space=pl.ANY)
    peaks = pl.pallas_call(
        functools.partial(fused_kernel, peers, block_len),
        out_shape=pltpu.VMEM((widths.shape[0], dms), jnp.float32),
        in_specs=[anywhere] * 4,
        out_specs=pl.BlockSpec(memory_space=pltpu.VMEM),
        scratch_shapes=[
            pltpu.VMEM(data.shape, data.dtype),
            pltpu.VMEM(chan_delay.shape, chan_delay.dtype),
            pltpu.VMEM(sub_delay.shape, sub_delay.dtype),
            pltpu.SMEM(widths.shape, widths.dtype),
            pltpu.SemaphoreType.DMA((4,)),
            pltpu.VMEM((bands, highs * NSDM, LOWS * CPS), jnp.bfloat16),
            pltpu.VMEM((bands, LOWS * CPS, block_len), jnp.bfloat16),
            pltpu.VMEM((2, sub_highs * dms, LOWS * rows // 2), jnp.bfloat16),
            pltpu.VMEM((2, LOWS * rows // 2, block_len), jnp.bfloat16),
            pltpu.VMEM((peers, group, block_len), jnp.bfloat16),
            pltpu.VMEM((peers, group, block_len), jnp.bfloat16),
            pltpu.VMEM((block_len, 2 * dms), jnp.float32),
            pltpu.SemaphoreType.DMA,
            pltpu.SemaphoreType.DMA((4,)),
        ],
        compiler_params=pltpu.CompilerParams(collective_id=0, has_side_effects=True),
    )(data, chan_delay, sub_delay, widths)
    return peaks.T


def solution(mesh):
    in_specs = (P(("beam", "freq"), "tm"), P(None, "freq"), P("freq", None), P())
    out_specs = P(("beam", "freq"), None)
    whole_time = mesh.shape["tm"] == 1
    return jax.shard_map(
        fused if whole_time else on_device, mesh=mesh, in_specs=in_specs, out_specs=out_specs, check_vma=False
    )
```

```python
import functools

import jax
import jax.numpy as jnp
from jax import lax
from jax.experimental import pallas as pl
from jax.experimental.pallas import tpu as pltpu
from jax.sharding import PartitionSpec as P

NSUB = 64
NSDM = 64
WMAX = 256
CPS = 64
DPS = 32
D1MAX = 40
D2MAX = 24


def passed_along(value, axis, steps):
    count = lax.axis_size(axis)
    initial, last = (max(0, -steps), min(count, count - steps))
    return lax.ppermute(value, axis, [(source, source + steps) for source in range(initial, last)])


def shifted_sum(source, delays, length, largest):
    band_count = source.shape[0]
    trial_count = delays.shape[1]
    start_total = jnp.zeros((band_count, trial_count, length), jnp.float32)

    def add_shifts(step_index, running_total):
        for within in range(2):
            offset = 2 * step_index + within
            window = lax.dynamic_slice_in_dim(source, offset, length, 2)
            selector = (delays == offset).astype(jnp.bfloat16)
            running_total = running_total + jnp.einsum(
                "bsm,bmt->bst", selector, window, preferred_element_type=jnp.float32
            )
        return running_total

    return lax.fori_loop(0, (largest + 2) // 2, add_shifts, start_total)


def form_subbands(extended, chan_delay, length):
    band_count = extended.shape[0] // CPS
    channel_slabs = extended.reshape(band_count, CPS, extended.shape[1])
    trial_delays = chan_delay.reshape(NSDM, band_count, CPS).transpose(1, 0, 2)
    return shifted_sum(channel_slabs, trial_delays, length, D1MAX).astype(jnp.bfloat16)


def prefix_sums(values):
    step = 1
    while step < values.shape[1]:
        values = values + jnp.pad(values[:, :-step], ((0, 0), (step, 0)))
        step *= 2
    return values


def peak_scores(normed, widths, span):
    running = jnp.concatenate([jnp.zeros((normed.shape[0], 1), normed.dtype), prefix_sums(normed)], axis=1)

    def one_width(width):
        upper = lax.dynamic_slice_in_dim(running, width, span, 1)
        return jnp.max((upper - running[:, :span]) / jnp.sqrt(width.astype(jnp.float32)), axis=1)

    return lax.map(one_width, widths).T


def on_device(data, chan_delay, sub_delay, widths):
    block_len = data.shape[1]
    total_len = block_len * lax.axis_size("tm")
    edge_rows = passed_along(data[:, :D1MAX], "tm", -1)
    extended = jnp.concatenate([data, edge_rows], axis=1)
    subband = form_subbands(extended, chan_delay, block_len)
    regrouped = lax.all_to_all(subband, "freq", split_axis=1, concat_axis=0, tiled=True)
    later = passed_along(regrouped[:, :, : D2MAX + WMAX], "tm", -1)
    regrouped = jnp.concatenate([regrouped, later], axis=2)
    dm_len = block_len + WMAX
    local_trials = regrouped.shape[1]
    grouped = sub_delay.reshape(local_trials, DPS, NSUB)
    by_trial = jnp.transpose(regrouped, (1, 0, 2))
    series = shifted_sum(by_trial, grouped, dm_len, D2MAX)
    series = series.reshape(local_trials * DPS, dm_len)
    inside = series[:, :block_len]
    totals = lax.psum(jnp.sum(inside, axis=1), "tm")
    average = totals / total_len
    centred = lax.psum(jnp.sum((inside - average[:, None]) ** 2, axis=1), "tm")
    spread = centred / total_len
    deviation = jnp.sqrt(spread + 1e-05)
    normed = (series - average[:, None]) / deviation[:, None]
    local_peaks = peak_scores(normed, widths, block_len)
    return lax.pmax(local_peaks, "tm")

LOWS = 4


def fused_kernel(peers, block_len, data_hbm, chan_hbm, sub_hbm, width_hbm, out_ref,
                 data_ref, chan_ref, sub_ref, width_ref, load_sem, select, shifted, picks, moved, outgoing, incoming,
                 running, send_sem, recv_sem):
    me = lax.axis_index("freq")
    rows = data_ref.shape[0]
    bands = rows // CPS
    own_trials = NSDM // peers
    dms = sub_ref.shape[0]
    group = bands * own_trials
    f32, bf16 = jnp.float32, jnp.bfloat16
    highs = D1MAX // LOWS + 1
    sub_highs = D2MAX // LOWS + 1
    blocks = block_len // 128

    loads = [
        pltpu.make_async_copy(source, target, load_sem.at[index])
        for index, (source, target) in enumerate((
            (chan_hbm, chan_ref), (data_hbm, data_ref), (sub_hbm, sub_ref), (width_hbm, width_ref)))
    ]
    for load in loads:
        load.start()

    barrier = pltpu.get_barrier_semaphore()

    def greet(step, carry):
        pl.semaphore_signal(barrier, inc=1, device_id={"freq": lax.rem(me + step, peers)},
                            device_id_type=pl.DeviceIdType.MESH)
        return carry

    lax.fori_loop(1, peers, greet, 0)

    def iota(shape, axis):
        return lax.broadcasted_iota(jnp.int32, shape, axis)

    def shift_rows(block, target, first, count):
        wide = block.astype(f32)
        lane = iota(wide.shape, 1)
        for low in range(LOWS):
            piece = wide
            if low:
                piece = jnp.where(lane < block_len - low, pltpu.roll(wide, block_len - low, 1), 0.0)
            target[low * count + first:low * count + first + wide.shape[0], :] = piece.astype(bf16)

    def total_of(product, count, count_highs):
        lane = iota((count, 128), 1)
        sums = [product[0:count, 128 * i:128 * (i + 1)] for i in range(blocks)]
        for high in range(1, count_highs):
            step = LOWS * high
            turned = [
                pltpu.roll(product[high * count:(high + 1) * count, 128 * i:128 * (i + 1)], 128 - step, 1)
                for i in range(blocks)
            ] + [0.0]
            for i in range(blocks):
                sums[i] = sums[i] + jnp.where(lane < 128 - step, turned[i], turned[i + 1])
        return sums

    def pick_trials(first, count):
        lane = iota((count, rows), 1)
        chan = chan_ref[first:first + count, :]
        other = pltpu.roll(chan, CPS, 1)
        for band in range(bands):
            near, far = (chan, other) if band == 0 else (other, chan)
            pair = jnp.where(lane < CPS, near, far - 1)
            for high in range(highs):
                for half in range(LOWS // 2):
                    block = jnp.where(pair == LOWS * high + 2 * half, 1.0, 0.0).astype(bf16)
                    start = highs * first + high * count
                    select[band, start:start + count, 128 * half:128 * (half + 1)] = block

    def form(first, count):
        for band in range(bands):
            start = highs * first
            product = jnp.dot(select[band, start:start + highs * count, :], shifted[band],
                              preferred_element_type=f32)
            sums = total_of(product, count, highs)
            for i in range(blocks):
                outgoing[first // own_trials:(first + count) // own_trials, own_trials * band:own_trials * (band + 1),
                         128 * i:128 * (i + 1)] = sums[i].astype(bf16).reshape(count // own_trials, own_trials, 128)

    quarter = peers // 4

    def sending(target):
        return pltpu.make_async_remote_copy(
            src_ref=outgoing.at[target], dst_ref=incoming.at[me],
            send_sem=send_sem, recv_sem=recv_sem.at[me // quarter],
            device_id={"freq": target}, device_id_type=pl.DeviceIdType.MESH)

    def start_one(target, carry):
        @pl.when(target != me)
        def _():
            sending(target).start()
        return carry

    first_trials = NSDM // 4
    loads[0].wait()
    pick_trials(0, first_trials)
    loads[1].wait()
    for band in range(bands):
        shift_rows(data_ref[band * CPS:(band + 1) * CPS, :], shifted.at[band], 0, CPS)
    form(0, first_trials)
    pick_trials(first_trials, NSDM - first_trials)
    form(first_trials, NSDM - first_trials)
    pl.semaphore_wait(barrier, peers - 1)
    lax.fori_loop(0, peers, start_one, 0)
    own = pltpu.make_async_copy(outgoing.at[me], incoming.at[me], recv_sem.at[me // quarter])
    own.start()

    loads[2].wait()
    loads[3].wait()
    trial_dms = dms // own_trials
    half_rows = rows // 2
    sub = sub_ref[...].astype(f32).astype(bf16)
    for half in range(2):
        lane = iota((NSUB, 128), 1)
        row = half * half_rows + lane % half_rows
        spread = (row // own_trials == iota((NSUB, 128), 0)).astype(f32).astype(bf16)
        delay = jnp.dot(sub, spread, preferred_element_type=f32)
        lane = iota((dms, 128), 1)
        delay = delay - (lane // half_rows).astype(f32)
        delay = jnp.where(lane % own_trials == iota((dms, 128), 0) // trial_dms, delay, -99.0)
        for high in range(sub_highs):
            for pair in range(LOWS // 2):
                picks[half, high * dms:(high + 1) * dms, 128 * pair:128 * (pair + 1)] = jnp.where(
                    delay == float(LOWS * high + 2 * pair), 1.0, 0.0).astype(bf16)
    below = (iota((136, 256), 1) % 128 < iota((136, 256), 0)).astype(f32).astype(bf16)

    def arrived(index):
        part = incoming.at[index * quarter:(index + 1) * quarter]
        pltpu.make_async_copy(part, part, recv_sem.at[index]).wait()
        block = jnp.concatenate(
            [incoming[index * quarter:(index + 1) * quarter, :, 128 * i:128 * (i + 1)].reshape(rows // 4, 128)
             for i in range(blocks)], axis=1)
        shift_rows(block, moved.at[index // 2], index % 2 * (rows // 4), half_rows)

    def half_series(half):
        product = jnp.dot(picks[half], moved[half], preferred_element_type=f32)
        return total_of(product, dms, sub_highs)

    arrived(0)
    arrived(1)
    early = half_series(0)
    arrived(2)
    arrived(3)
    late = half_series(1)

    series = [a + b for a, b in zip(early, late)]
    average = jnp.sum(sum(series), axis=1, keepdims=True) / block_len
    centred = [block - average for block in series]
    spread = jnp.sum(sum(block * block for block in centred), axis=1, keepdims=True) / block_len
    deviation = jnp.sqrt(spread + 1e-05)
    across = jnp.broadcast_to(deviation, (dms, 128)).T[0:1, :]
    centred = centred + [jnp.broadcast_to(-average, (dms, 128))] * (WMAX // 128)
    heads = [block.astype(bf16) for block in centred]
    tails = [(block - head.astype(f32)).astype(bf16) for block, head in zip(centred, heads)]
    ahead = blocks + WMAX // 128 - blocks
    carry = jnp.zeros((1, 2 * dms), f32)
    for i in range(blocks):
        j = i + 2
        block = jnp.concatenate([
            jnp.concatenate([heads[i], tails[i]], axis=1), jnp.concatenate([heads[j], tails[j]], axis=1)], axis=0)
        sums = lax.dot_general(below, block, (((1,), (1,)), ((), ())), preferred_element_type=f32)
        running[128 * i:128 * (i + 1), :] = sums[0:128, :] + carry
        carry = carry + sums[128:129, :]

    span = block_len - 256
    base = running[0:span, :]
    peaks = []
    for index in range(width_ref.shape[0]):
        width = width_ref[index]
        upper = running[pl.ds(width, span), :]
        peaks.append(jnp.max(upper - base, axis=0, keepdims=True))
    peaks = jnp.concatenate(peaks, axis=0)
    peaks = jnp.maximum(peaks, pltpu.roll(peaks, dms, 1))
    scales = jnp.concatenate(
        [jnp.full((1, dms), width_ref[index].astype(f32)) for index in range(width_ref.shape[0])], axis=0)
    out_ref[...] = peaks[:, 0:dms] / (across * jnp.sqrt(scales))
    sent = outgoing.at[0:peers - 1]
    pltpu.make_async_copy(sent, sent, send_sem).wait()


def fused(data, chan_delay, sub_delay, widths):
    peers = lax.axis_size("freq")
    rows, block_len = data.shape
    bands = rows // CPS
    dms = sub_delay.shape[0]
    group = bands * (NSDM // peers)
    highs = D1MAX // LOWS + 1
    sub_highs = D2MAX // LOWS + 1
    anywhere = pl.BlockSpec(memory_space=pl.ANY)
    peaks = pl.pallas_call(
        functools.partial(fused_kernel, peers, block_len),
        out_shape=pltpu.VMEM((widths.shape[0], dms), jnp.float32),
        in_specs=[anywhere] * 4,
        out_specs=pl.BlockSpec(memory_space=pltpu.VMEM),
        scratch_shapes=[
            pltpu.VMEM(data.shape, data.dtype),
            pltpu.VMEM(chan_delay.shape, chan_delay.dtype),
            pltpu.VMEM(sub_delay.shape, sub_delay.dtype),
            pltpu.SMEM(widths.shape, widths.dtype),
            pltpu.SemaphoreType.DMA((4,)),
            pltpu.VMEM((bands, highs * NSDM, LOWS * CPS), jnp.bfloat16),
            pltpu.VMEM((bands, LOWS * CPS, block_len), jnp.bfloat16),
            pltpu.VMEM((2, sub_highs * dms, LOWS * rows // 2), jnp.bfloat16),
            pltpu.VMEM((2, LOWS * rows // 2, block_len), jnp.bfloat16),
            pltpu.VMEM((peers, group, block_len), jnp.bfloat16),
            pltpu.VMEM((peers, group, block_len), jnp.bfloat16),
            pltpu.VMEM((block_len, 2 * dms), jnp.float32),
            pltpu.SemaphoreType.DMA,
            pltpu.SemaphoreType.DMA((4,)),
        ],
        compiler_params=pltpu.CompilerParams(collective_id=0, has_side_effects=True),
    )(data, chan_delay, sub_delay, widths)
    return peaks.T


def solution(mesh):
    in_specs = (P(("beam", "freq"), "tm"), P(None, "freq"), P("freq", None), P())
    out_specs = P(("beam", "freq"), None)
    whole_time = mesh.shape["tm"] == 1
    return jax.shard_map(
        fused if whole_time else on_device, mesh=mesh, in_specs=in_specs, out_specs=out_specs, check_vma=False
    )
```

```python
import functools

import jax
import jax.numpy as jnp
from jax import lax
from jax.experimental import pallas as pl
from jax.experimental.pallas import tpu as pltpu
from jax.sharding import PartitionSpec as P

NSUB = 64
NSDM = 64
WMAX = 256
CPS = 64
DPS = 32
D1MAX = 40
D2MAX = 24


def passed_along(value, axis, steps):
    count = lax.axis_size(axis)
    initial, last = (max(0, -steps), min(count, count - steps))
    return lax.ppermute(value, axis, [(source, source + steps) for source in range(initial, last)])


def shifted_sum(source, delays, length, largest):
    band_count = source.shape[0]
    trial_count = delays.shape[1]
    start_total = jnp.zeros((band_count, trial_count, length), jnp.float32)

    def add_shifts(step_index, running_total):
        for within in range(2):
            offset = 2 * step_index + within
            window = lax.dynamic_slice_in_dim(source, offset, length, 2)
            selector = (delays == offset).astype(jnp.bfloat16)
            running_total = running_total + jnp.einsum(
                "bsm,bmt->bst", selector, window, preferred_element_type=jnp.float32
            )
        return running_total

    return lax.fori_loop(0, (largest + 2) // 2, add_shifts, start_total)


def form_subbands(extended, chan_delay, length):
    band_count = extended.shape[0] // CPS
    channel_slabs = extended.reshape(band_count, CPS, extended.shape[1])
    trial_delays = chan_delay.reshape(NSDM, band_count, CPS).transpose(1, 0, 2)
    return shifted_sum(channel_slabs, trial_delays, length, D1MAX).astype(jnp.bfloat16)


def prefix_sums(values):
    step = 1
    while step < values.shape[1]:
        values = values + jnp.pad(values[:, :-step], ((0, 0), (step, 0)))
        step *= 2
    return values


def peak_scores(normed, widths, span):
    running = jnp.concatenate([jnp.zeros((normed.shape[0], 1), normed.dtype), prefix_sums(normed)], axis=1)

    def one_width(width):
        upper = lax.dynamic_slice_in_dim(running, width, span, 1)
        return jnp.max((upper - running[:, :span]) / jnp.sqrt(width.astype(jnp.float32)), axis=1)

    return lax.map(one_width, widths).T


def on_device(data, chan_delay, sub_delay, widths):
    block_len = data.shape[1]
    total_len = block_len * lax.axis_size("tm")
    edge_rows = passed_along(data[:, :D1MAX], "tm", -1)
    extended = jnp.concatenate([data, edge_rows], axis=1)
    subband = form_subbands(extended, chan_delay, block_len)
    regrouped = lax.all_to_all(subband, "freq", split_axis=1, concat_axis=0, tiled=True)
    later = passed_along(regrouped[:, :, : D2MAX + WMAX], "tm", -1)
    regrouped = jnp.concatenate([regrouped, later], axis=2)
    dm_len = block_len + WMAX
    local_trials = regrouped.shape[1]
    grouped = sub_delay.reshape(local_trials, DPS, NSUB)
    by_trial = jnp.transpose(regrouped, (1, 0, 2))
    series = shifted_sum(by_trial, grouped, dm_len, D2MAX)
    series = series.reshape(local_trials * DPS, dm_len)
    inside = series[:, :block_len]
    totals = lax.psum(jnp.sum(inside, axis=1), "tm")
    average = totals / total_len
    centred = lax.psum(jnp.sum((inside - average[:, None]) ** 2, axis=1), "tm")
    spread = centred / total_len
    deviation = jnp.sqrt(spread + 1e-05)
    normed = (series - average[:, None]) / deviation[:, None]
    local_peaks = peak_scores(normed, widths, block_len)
    return lax.pmax(local_peaks, "tm")

LOWS = 4


def fused_kernel(peers, block_len, data_hbm, chan_hbm, sub_hbm, width_hbm, out_ref,
                 data_ref, chan_ref, sub_ref, width_ref, load_sem, select, shifted, picks, moved, outgoing, incoming,
                 running, totals, send_sem, recv_sem):
    me = lax.axis_index("freq")
    rows = data_ref.shape[0]
    bands = rows // CPS
    own_trials = NSDM // peers
    dms = sub_ref.shape[0]
    group = bands * own_trials
    f32, bf16 = jnp.float32, jnp.bfloat16
    highs = D1MAX // LOWS + 1
    sub_highs = D2MAX // LOWS + 1
    blocks = block_len // 128

    loads = [
        pltpu.make_async_copy(source, target, load_sem.at[index])
        for index, (source, target) in enumerate((
            (chan_hbm, chan_ref), (data_hbm, data_ref), (sub_hbm, sub_ref), (width_hbm, width_ref)))
    ]
    for load in loads:
        load.start()

    barrier = pltpu.get_barrier_semaphore()

    def greet(step, carry):
        pl.semaphore_signal(barrier, inc=1, device_id={"freq": lax.rem(me + step, peers)},
                            device_id_type=pl.DeviceIdType.MESH)
        return carry

    lax.fori_loop(1, peers, greet, 0)

    def iota(shape, axis):
        return lax.broadcasted_iota(jnp.int32, shape, axis)

    def shift_rows(block, target, first, count):
        lane = iota(block.shape, 1)
        for low in range(LOWS):
            piece = block
            if low:
                piece = jnp.where(lane < block_len - low, pltpu.roll(block, block_len - low, 1), jnp.zeros_like(block))
            target[low * count + first:low * count + first + block.shape[0], :] = piece

    def total_of(product, count, count_highs):
        lane = iota((count, 128), 1)
        sums = [product[0:count, 128 * i:128 * (i + 1)] for i in range(blocks)]
        for high in range(1, count_highs):
            step = LOWS * high
            turned = [
                pltpu.roll(product[high * count:(high + 1) * count, 128 * i:128 * (i + 1)], 128 - step, 1)
                for i in range(blocks)
            ] + [0.0]
            for i in range(blocks):
                sums[i] = sums[i] + jnp.where(lane < 128 - step, turned[i], turned[i + 1])
        return sums

    def pick_trials(first, count):
        lane = iota((count, rows), 1)
        chan = chan_ref[first:first + count, :]
        other = pltpu.roll(chan, CPS, 1)
        for band in range(bands):
            near, far = (chan, other) if band == 0 else (other, chan)
            pair = jnp.where(lane < CPS, near, far - 1)
            for high in range(highs):
                for half in range(LOWS // 2):
                    block = jnp.where(pair == LOWS * high + 2 * half, 1.0, 0.0).astype(bf16)
                    start = highs * first + high * count
                    select[band, start:start + count, 128 * half:128 * (half + 1)] = block

    def form(first, count):
        for band in range(bands):
            start = highs * first
            product = jnp.dot(select[band, start:start + highs * count, :], shifted[band],
                              preferred_element_type=f32)
            sums = total_of(product, count, highs)
            for i in range(blocks):
                outgoing[first // own_trials:(first + count) // own_trials, own_trials * band:own_trials * (band + 1),
                         128 * i:128 * (i + 1)] = sums[i].astype(bf16).reshape(count // own_trials, own_trials, 128)

    quarter = peers // 4

    def sending(target):
        return pltpu.make_async_remote_copy(
            src_ref=outgoing.at[target], dst_ref=incoming.at[me],
            send_sem=send_sem, recv_sem=recv_sem.at[me // quarter],
            device_id={"freq": target}, device_id_type=pl.DeviceIdType.MESH)

    def start_one(target, carry):
        @pl.when(target != me)
        def _():
            sending(target).start()
        return carry

    first_trials = NSDM // 4
    loads[0].wait()
    pick_trials(0, first_trials)
    loads[1].wait()
    for band in range(bands):
        shift_rows(data_ref[band * CPS:(band + 1) * CPS, :], shifted.at[band], 0, CPS)
    form(0, first_trials)
    pick_trials(first_trials, NSDM - first_trials)
    form(first_trials, NSDM - first_trials)
    pl.semaphore_wait(barrier, peers - 1)
    lax.fori_loop(0, peers, start_one, 0)
    own = pltpu.make_async_copy(outgoing.at[me], incoming.at[me], recv_sem.at[me // quarter])
    own.start()

    loads[2].wait()
    loads[3].wait()
    trial_dms = dms // own_trials
    half_rows = rows // 2
    sub = sub_ref[...].astype(f32).astype(bf16)
    for half in range(2):
        lane = iota((NSUB, 128), 1)
        row = half * half_rows + lane % half_rows
        spread = (row // own_trials == iota((NSUB, 128), 0)).astype(f32).astype(bf16)
        delay = jnp.dot(sub, spread, preferred_element_type=f32)
        lane = iota((dms, 128), 1)
        delay = delay - (lane // half_rows).astype(f32)
        delay = jnp.where(lane % own_trials == iota((dms, 128), 0) // trial_dms, delay, -99.0)
        for high in range(sub_highs):
            for pair in range(LOWS // 2):
                picks[half, high * dms:(high + 1) * dms, 128 * pair:128 * (pair + 1)] = jnp.where(
                    delay == float(LOWS * high + 2 * pair), 1.0, 0.0).astype(bf16)
    before = jnp.where(iota((256, 256), 1) < 128, iota((256, 256), 0) % 128 - iota((256, 256), 1), -1) < 0
    totals[...] = before.astype(f32).astype(bf16)

    def arrived(index, place):
        part = incoming.at[pl.ds(index * quarter, quarter)]
        pltpu.make_async_copy(part, part, recv_sem.at[index]).wait()
        block = jnp.concatenate(
            [incoming[pl.ds(index * quarter, quarter), :, 128 * i:128 * (i + 1)].reshape(rows // 4, 128)
             for i in range(blocks)], axis=1)
        shift_rows(block, moved.at[index // 2], place * (rows // 4), half_rows)

    def half_series(half):
        arrived(2 * half, 0)
        arrived(2 * half + 1, 1)
        return total_of(jnp.dot(picks[half], moved[half], preferred_element_type=f32), dms, sub_highs)

    near = (2 * me) // peers
    series = [a + b for a, b in zip(half_series(near), half_series(1 - near))]
    average = jnp.sum(sum(series), axis=1, keepdims=True) / block_len
    centred = [block - average for block in series]
    spread = jnp.sum(sum(block * block for block in centred), axis=1, keepdims=True) / block_len
    deviation = jnp.sqrt(spread + 1e-05)
    across = jnp.broadcast_to(deviation, (dms, 128)).T[0:1, :]
    stacked = jnp.concatenate(centred, axis=0)
    head = stacked.astype(bf16)
    tail = (stacked - head.astype(f32)).astype(bf16)
    sums = jnp.dot(jnp.concatenate([head, tail], axis=1), totals[...], preferred_element_type=f32)
    carry = jnp.zeros((dms, 128), f32)
    pieces = []
    for i in range(blocks):
        block = sums[i * dms:(i + 1) * dms, :]
        pieces.append(block[:, 0:128] + carry)
        carry = carry + block[:, 128:256]
    for i in range(WMAX // 128):
        pieces.append(carry - average * (iota((dms, 128), 1) + 128 * i).astype(f32))
    for i in range(blocks):
        running[128 * i:128 * (i + 1), :] = jnp.concatenate([pieces[i], pieces[i + 2]], axis=0).T

    span = block_len - 256
    tile = 64
    count = width_ref.shape[0]
    widths = [width_ref[index] for index in range(count)]
    best = [None] * count
    for start in range(0, span, tile):
        base = running[start:start + tile, :]
        for index in range(count):
            rise = running[pl.ds(widths[index] + start, tile), :] - base
            rise = jnp.max(rise.reshape(tile // 8, 8, 2 * dms), axis=0)
            best[index] = rise if start == 0 else jnp.maximum(best[index], rise)
    peaks = [jnp.max(rise, axis=0, keepdims=True) for rise in best]
    peaks = jnp.concatenate(peaks, axis=0)
    peaks = jnp.maximum(peaks, pltpu.roll(peaks, dms, 1))
    scales = jnp.concatenate(
        [jnp.full((1, dms), width_ref[index].astype(f32)) for index in range(width_ref.shape[0])], axis=0)
    out_ref[...] = peaks[:, 0:dms] / (across * jnp.sqrt(scales))
    sent = outgoing.at[0:peers - 1]
    pltpu.make_async_copy(sent, sent, send_sem).wait()


def fused(data, chan_delay, sub_delay, widths):
    peers = lax.axis_size("freq")
    rows, block_len = data.shape
    bands = rows // CPS
    dms = sub_delay.shape[0]
    group = bands * (NSDM // peers)
    highs = D1MAX // LOWS + 1
    sub_highs = D2MAX // LOWS + 1
    anywhere = pl.BlockSpec(memory_space=pl.ANY)
    peaks = pl.pallas_call(
        functools.partial(fused_kernel, peers, block_len),
        out_shape=pltpu.VMEM((widths.shape[0], dms), jnp.float32),
        in_specs=[anywhere] * 4,
        out_specs=pl.BlockSpec(memory_space=pltpu.VMEM),
        scratch_shapes=[
            pltpu.VMEM(data.shape, data.dtype),
            pltpu.VMEM(chan_delay.shape, chan_delay.dtype),
            pltpu.VMEM(sub_delay.shape, sub_delay.dtype),
            pltpu.SMEM(widths.shape, widths.dtype),
            pltpu.SemaphoreType.DMA((4,)),
            pltpu.VMEM((bands, highs * NSDM, LOWS * CPS), jnp.bfloat16),
            pltpu.VMEM((bands, LOWS * CPS, block_len), jnp.bfloat16),
            pltpu.VMEM((2, sub_highs * dms, LOWS * rows // 2), jnp.bfloat16),
            pltpu.VMEM((2, LOWS * rows // 2, block_len), jnp.bfloat16),
            pltpu.VMEM((peers, group, block_len), jnp.bfloat16),
            pltpu.VMEM((peers, group, block_len), jnp.bfloat16),
            pltpu.VMEM((block_len, 2 * dms), jnp.float32),
            pltpu.VMEM((256, 256), jnp.bfloat16),
            pltpu.SemaphoreType.DMA,
            pltpu.SemaphoreType.DMA((4,)),
        ],
        compiler_params=pltpu.CompilerParams(collective_id=0, has_side_effects=True),
    )(data, chan_delay, sub_delay, widths)
    return peaks.T


def solution(mesh):
    in_specs = (P(("beam", "freq"), "tm"), P(None, "freq"), P("freq", None), P())
    out_specs = P(("beam", "freq"), None)
    whole_time = mesh.shape["tm"] == 1
    return jax.shard_map(
        fused if whole_time else on_device, mesh=mesh, in_specs=in_specs, out_specs=out_specs, check_vma=False
    )
```

```python
import functools

import jax
import jax.numpy as jnp
from jax import lax
from jax.experimental import pallas as pl
from jax.experimental.pallas import tpu as pltpu
from jax.sharding import PartitionSpec as P

NSUB = 64
NSDM = 64
WMAX = 256
CPS = 64
DPS = 32
D1MAX = 40
D2MAX = 24


def passed_along(value, axis, steps):
    count = lax.axis_size(axis)
    initial, last = (max(0, -steps), min(count, count - steps))
    return lax.ppermute(value, axis, [(source, source + steps) for source in range(initial, last)])


def shifted_sum(source, delays, length, largest):
    band_count = source.shape[0]
    trial_count = delays.shape[1]
    start_total = jnp.zeros((band_count, trial_count, length), jnp.float32)

    def add_shifts(step_index, running_total):
        for within in range(2):
            offset = 2 * step_index + within
            window = lax.dynamic_slice_in_dim(source, offset, length, 2)
            selector = (delays == offset).astype(jnp.bfloat16)
            running_total = running_total + jnp.einsum(
                "bsm,bmt->bst", selector, window, preferred_element_type=jnp.float32
            )
        return running_total

    return lax.fori_loop(0, (largest + 2) // 2, add_shifts, start_total)


def form_subbands(extended, chan_delay, length):
    band_count = extended.shape[0] // CPS
    channel_slabs = extended.reshape(band_count, CPS, extended.shape[1])
    trial_delays = chan_delay.reshape(NSDM, band_count, CPS).transpose(1, 0, 2)
    return shifted_sum(channel_slabs, trial_delays, length, D1MAX).astype(jnp.bfloat16)


def prefix_sums(values):
    step = 1
    while step < values.shape[1]:
        values = values + jnp.pad(values[:, :-step], ((0, 0), (step, 0)))
        step *= 2
    return values


def peak_scores(normed, widths, span):
    running = jnp.concatenate([jnp.zeros((normed.shape[0], 1), normed.dtype), prefix_sums(normed)], axis=1)

    def one_width(width):
        upper = lax.dynamic_slice_in_dim(running, width, span, 1)
        return jnp.max((upper - running[:, :span]) / jnp.sqrt(width.astype(jnp.float32)), axis=1)

    return lax.map(one_width, widths).T


def on_device(data, chan_delay, sub_delay, widths):
    block_len = data.shape[1]
    total_len = block_len * lax.axis_size("tm")
    edge_rows = passed_along(data[:, :D1MAX], "tm", -1)
    extended = jnp.concatenate([data, edge_rows], axis=1)
    subband = form_subbands(extended, chan_delay, block_len)
    regrouped = lax.all_to_all(subband, "freq", split_axis=1, concat_axis=0, tiled=True)
    later = passed_along(regrouped[:, :, : D2MAX + WMAX], "tm", -1)
    regrouped = jnp.concatenate([regrouped, later], axis=2)
    dm_len = block_len + WMAX
    local_trials = regrouped.shape[1]
    grouped = sub_delay.reshape(local_trials, DPS, NSUB)
    by_trial = jnp.transpose(regrouped, (1, 0, 2))
    series = shifted_sum(by_trial, grouped, dm_len, D2MAX)
    series = series.reshape(local_trials * DPS, dm_len)
    inside = series[:, :block_len]
    totals = lax.psum(jnp.sum(inside, axis=1), "tm")
    average = totals / total_len
    centred = lax.psum(jnp.sum((inside - average[:, None]) ** 2, axis=1), "tm")
    spread = centred / total_len
    deviation = jnp.sqrt(spread + 1e-05)
    normed = (series - average[:, None]) / deviation[:, None]
    local_peaks = peak_scores(normed, widths, block_len)
    return lax.pmax(local_peaks, "tm")

LOWS = 4


def fused_kernel(peers, block_len, data_hbm, chan_hbm, sub_hbm, width_hbm, out_ref,
                 data_ref, chan_ref, sub_ref, width_ref, load_sem, select, shifted, picks, moved, outgoing, incoming,
                 running, totals, send_sem, recv_sem):
    me = lax.axis_index("freq")
    rows = data_ref.shape[0]
    bands = rows // CPS
    own_trials = NSDM // peers
    dms = sub_ref.shape[0]
    group = bands * own_trials
    f32, bf16 = jnp.float32, jnp.bfloat16
    highs = D1MAX // LOWS + 1
    sub_highs = D2MAX // LOWS + 1
    blocks = block_len // 128

    loads = [
        pltpu.make_async_copy(source, target, load_sem.at[index])
        for index, (source, target) in enumerate((
            (chan_hbm, chan_ref), (data_hbm, data_ref), (sub_hbm, sub_ref), (width_hbm, width_ref)))
    ]
    for load in loads:
        load.start()

    barrier = pltpu.get_barrier_semaphore()

    def greet(step, carry):
        pl.semaphore_signal(barrier, inc=1, device_id={"freq": lax.rem(me + step, peers)},
                            device_id_type=pl.DeviceIdType.MESH)
        return carry

    lax.fori_loop(1, peers, greet, 0)

    def iota(shape, axis):
        return lax.broadcasted_iota(jnp.int32, shape, axis)

    def shift_rows(block, target, first, count):
        lane = iota(block.shape, 1)
        for low in range(LOWS):
            piece = block
            if low:
                piece = jnp.where(lane < block_len - low, pltpu.roll(block, block_len - low, 1), jnp.zeros_like(block))
            target[low * count + first:low * count + first + block.shape[0], :] = piece

    def total_of(product, count, count_highs):
        lane = iota((count, 128), 1)
        sums = [product[0:count, 128 * i:128 * (i + 1)] for i in range(blocks)]
        for high in range(1, count_highs):
            step = LOWS * high
            turned = [
                pltpu.roll(product[high * count:(high + 1) * count, 128 * i:128 * (i + 1)], 128 - step, 1)
                for i in range(blocks)
            ] + [0.0]
            for i in range(blocks):
                sums[i] = sums[i] + jnp.where(lane < 128 - step, turned[i], turned[i + 1])
        return sums

    def pick_trials(first, count):
        lane = iota((count, rows), 1)
        chan = chan_ref[first:first + count, :]
        other = pltpu.roll(chan, CPS, 1)
        for band in range(bands):
            near, far = (chan, other) if band == 0 else (other, chan)
            pair = jnp.where(lane < CPS, near, far - 1)
            for high in range(highs):
                for half in range(LOWS // 2):
                    block = jnp.where(pair == LOWS * high + 2 * half, 1.0, 0.0).astype(bf16)
                    start = highs * first + high * count
                    select[band, start:start + count, 128 * half:128 * (half + 1)] = block

    def form(first, count):
        for band in range(bands):
            start = highs * first
            product = jnp.dot(select[band, start:start + highs * count, :], shifted[band],
                              preferred_element_type=f32)
            sums = total_of(product, count, highs)
            for i in range(blocks):
                outgoing[first // own_trials:(first + count) // own_trials, own_trials * band:own_trials * (band + 1),
                         128 * i:128 * (i + 1)] = sums[i].astype(bf16).reshape(count // own_trials, own_trials, 128)

    quarter = peers // 4

    def sending(target):
        return pltpu.make_async_remote_copy(
            src_ref=outgoing.at[target], dst_ref=incoming.at[me],
            send_sem=send_sem, recv_sem=recv_sem.at[me // quarter],
            device_id={"freq": target}, device_id_type=pl.DeviceIdType.MESH)

    def start_one(target, carry):
        @pl.when(target != me)
        def _():
            sending(target).start()
        return carry

    first_trials = NSDM // 4
    loads[0].wait()
    pick_trials(0, first_trials)
    loads[1].wait()
    for band in range(bands):
        shift_rows(data_ref[band * CPS:(band + 1) * CPS, :], shifted.at[band], 0, CPS)
    form(0, first_trials)
    last = me >= peers - 2

    def meet():
        pl.semaphore_wait(barrier, peers - 1)
        lax.fori_loop(0, 2, start_one, 0)

    pl.when(last)(meet)
    pick_trials(first_trials, NSDM - first_trials)
    form(first_trials, NSDM - first_trials)
    pl.when(jnp.logical_not(last))(meet)

    def start_rest(step, carry):
        target = lax.rem(me + step, peers)
        @pl.when(target >= 2)
        def _():
            start_one(target, carry)
        return carry

    lax.fori_loop(0, peers, start_rest, 0)
    own = pltpu.make_async_copy(outgoing.at[me], incoming.at[me], recv_sem.at[me // quarter])
    own.start()

    loads[2].wait()
    loads[3].wait()
    trial_dms = dms // own_trials
    half_rows = rows // 2
    sub = sub_ref[...].astype(f32).astype(bf16)
    for half in range(2):
        lane = iota((NSUB, 128), 1)
        row = half * half_rows + lane % half_rows
        spread = (row // own_trials == iota((NSUB, 128), 0)).astype(f32).astype(bf16)
        delay = jnp.dot(sub, spread, preferred_element_type=f32)
        lane = iota((dms, 128), 1)
        delay = delay - (lane // half_rows).astype(f32)
        delay = jnp.where(lane % own_trials == iota((dms, 128), 0) // trial_dms, delay, -99.0)
        for high in range(sub_highs):
            for pair in range(LOWS // 2):
                picks[half, high * dms:(high + 1) * dms, 128 * pair:128 * (pair + 1)] = jnp.where(
                    delay == float(LOWS * high + 2 * pair), 1.0, 0.0).astype(bf16)
    before = jnp.where(iota((256, 256), 1) < 128, iota((256, 256), 0) % 128 - iota((256, 256), 1), -1) < 0
    totals[...] = before.astype(f32).astype(bf16)

    def arrived(index, place):
        part = incoming.at[pl.ds(index * quarter, quarter)]
        pltpu.make_async_copy(part, part, recv_sem.at[index]).wait()
        block = jnp.concatenate(
            [incoming[pl.ds(index * quarter, quarter), :, 128 * i:128 * (i + 1)].reshape(rows // 4, 128)
             for i in range(blocks)], axis=1)
        shift_rows(block, moved.at[index // 2], place * (rows // 4), half_rows)

    def half_series(half):
        arrived(2 * half, 0)
        arrived(2 * half + 1, 1)
        return total_of(jnp.dot(picks[half], moved[half], preferred_element_type=f32), dms, sub_highs)

    near = (2 * me) // peers
    series = [a + b for a, b in zip(half_series(near), half_series(1 - near))]
    average = jnp.sum(sum(series), axis=1, keepdims=True) / block_len
    centred = [block - average for block in series]
    spread = jnp.sum(sum(block * block for block in centred), axis=1, keepdims=True) / block_len
    deviation = jnp.sqrt(spread + 1e-05)
    across = jnp.broadcast_to(deviation, (dms, 128)).T[0:1, :]
    stacked = jnp.concatenate(centred, axis=0)
    head = stacked.astype(bf16)
    tail = (stacked - head.astype(f32)).astype(bf16)
    sums = jnp.dot(jnp.concatenate([head, tail], axis=1), totals[...], preferred_element_type=f32)
    carry = jnp.zeros((dms, 128), f32)
    pieces = []
    for i in range(blocks):
        block = sums[i * dms:(i + 1) * dms, :]
        pieces.append(block[:, 0:128] + carry)
        carry = carry + block[:, 128:256]
    for i in range(WMAX // 128):
        pieces.append(carry - average * (iota((dms, 128), 1) + 128 * i).astype(f32))
    for i in range(blocks):
        running[128 * i:128 * (i + 1), :] = jnp.concatenate([pieces[i], pieces[i + 2]], axis=0).T

    span = block_len - 256
    tile = 64
    count = width_ref.shape[0]
    widths = [width_ref[index] for index in range(count)]
    best = [None] * count
    for start in range(0, span, tile):
        base = running[start:start + tile, :]
        for index in range(count):
            rise = running[pl.ds(widths[index] + start, tile), :] - base
            rise = jnp.max(rise.reshape(tile // 8, 8, 2 * dms), axis=0)
            best[index] = rise if start == 0 else jnp.maximum(best[index], rise)
    peaks = [jnp.max(rise, axis=0, keepdims=True) for rise in best]
    peaks = jnp.concatenate(peaks, axis=0)
    peaks = jnp.maximum(peaks, pltpu.roll(peaks, dms, 1))
    scales = jnp.concatenate(
        [jnp.full((1, dms), width_ref[index].astype(f32)) for index in range(width_ref.shape[0])], axis=0)
    out_ref[...] = peaks[:, 0:dms] / (across * jnp.sqrt(scales))
    sent = outgoing.at[0:peers - 1]
    pltpu.make_async_copy(sent, sent, send_sem).wait()


def fused(data, chan_delay, sub_delay, widths):
    peers = lax.axis_size("freq")
    rows, block_len = data.shape
    bands = rows // CPS
    dms = sub_delay.shape[0]
    group = bands * (NSDM // peers)
    highs = D1MAX // LOWS + 1
    sub_highs = D2MAX // LOWS + 1
    anywhere = pl.BlockSpec(memory_space=pl.ANY)
    peaks = pl.pallas_call(
        functools.partial(fused_kernel, peers, block_len),
        out_shape=pltpu.VMEM((widths.shape[0], dms), jnp.float32),
        in_specs=[anywhere] * 4,
        out_specs=pl.BlockSpec(memory_space=pltpu.VMEM),
        scratch_shapes=[
            pltpu.VMEM(data.shape, data.dtype),
            pltpu.VMEM(chan_delay.shape, chan_delay.dtype),
            pltpu.VMEM(sub_delay.shape, sub_delay.dtype),
            pltpu.SMEM(widths.shape, widths.dtype),
            pltpu.SemaphoreType.DMA((4,)),
            pltpu.VMEM((bands, highs * NSDM, LOWS * CPS), jnp.bfloat16),
            pltpu.VMEM((bands, LOWS * CPS, block_len), jnp.bfloat16),
            pltpu.VMEM((2, sub_highs * dms, LOWS * rows // 2), jnp.bfloat16),
            pltpu.VMEM((2, LOWS * rows // 2, block_len), jnp.bfloat16),
            pltpu.VMEM((peers, group, block_len), jnp.bfloat16),
            pltpu.VMEM((peers, group, block_len), jnp.bfloat16),
            pltpu.VMEM((block_len, 2 * dms), jnp.float32),
            pltpu.VMEM((256, 256), jnp.bfloat16),
            pltpu.SemaphoreType.DMA,
            pltpu.SemaphoreType.DMA((4,)),
        ],
        compiler_params=pltpu.CompilerParams(collective_id=0, has_side_effects=True),
    )(data, chan_delay, sub_delay, widths)
    return peaks.T


def solution(mesh):
    in_specs = (P(("beam", "freq"), "tm"), P(None, "freq"), P("freq", None), P())
    out_specs = P(("beam", "freq"), None)
    whole_time = mesh.shape["tm"] == 1 and mesh.shape["freq"] % 8 == 0
    return jax.shard_map(
        fused if whole_time else on_device, mesh=mesh, in_specs=in_specs, out_specs=out_specs, check_vma=False
    )
```

```python
import functools

import jax
import jax.numpy as jnp
from jax import lax
from jax.experimental import pallas as pl
from jax.experimental.pallas import tpu as pltpu
from jax.sharding import PartitionSpec as P

NSUB = 64
NSDM = 64
WMAX = 256
CPS = 64
DPS = 32
D1MAX = 40
D2MAX = 24


def passed_along(value, axis, steps):
    count = lax.axis_size(axis)
    initial, last = (max(0, -steps), min(count, count - steps))
    return lax.ppermute(value, axis, [(source, source + steps) for source in range(initial, last)])


def shifted_sum(source, delays, length, largest):
    band_count = source.shape[0]
    trial_count = delays.shape[1]
    start_total = jnp.zeros((band_count, trial_count, length), jnp.float32)

    def add_shifts(step_index, running_total):
        for within in range(2):
            offset = 2 * step_index + within
            window = lax.dynamic_slice_in_dim(source, offset, length, 2)
            selector = (delays == offset).astype(jnp.bfloat16)
            running_total = running_total + jnp.einsum(
                "bsm,bmt->bst", selector, window, preferred_element_type=jnp.float32
            )
        return running_total

    return lax.fori_loop(0, (largest + 2) // 2, add_shifts, start_total)


def form_subbands(extended, chan_delay, length):
    band_count = extended.shape[0] // CPS
    channel_slabs = extended.reshape(band_count, CPS, extended.shape[1])
    trial_delays = chan_delay.reshape(NSDM, band_count, CPS).transpose(1, 0, 2)
    return shifted_sum(channel_slabs, trial_delays, length, D1MAX).astype(jnp.bfloat16)


def prefix_sums(values):
    step = 1
    while step < values.shape[1]:
        values = values + jnp.pad(values[:, :-step], ((0, 0), (step, 0)))
        step *= 2
    return values


def peak_scores(normed, widths, span):
    running = jnp.concatenate([jnp.zeros((normed.shape[0], 1), normed.dtype), prefix_sums(normed)], axis=1)

    def one_width(width):
        upper = lax.dynamic_slice_in_dim(running, width, span, 1)
        return jnp.max((upper - running[:, :span]) / jnp.sqrt(width.astype(jnp.float32)), axis=1)

    return lax.map(one_width, widths).T


def on_device(data, chan_delay, sub_delay, widths):
    block_len = data.shape[1]
    total_len = block_len * lax.axis_size("tm")
    edge_rows = passed_along(data[:, :D1MAX], "tm", -1)
    extended = jnp.concatenate([data, edge_rows], axis=1)
    subband = form_subbands(extended, chan_delay, block_len)
    regrouped = lax.all_to_all(subband, "freq", split_axis=1, concat_axis=0, tiled=True)
    later = passed_along(regrouped[:, :, : D2MAX + WMAX], "tm", -1)
    regrouped = jnp.concatenate([regrouped, later], axis=2)
    dm_len = block_len + WMAX
    local_trials = regrouped.shape[1]
    grouped = sub_delay.reshape(local_trials, DPS, NSUB)
    by_trial = jnp.transpose(regrouped, (1, 0, 2))
    series = shifted_sum(by_trial, grouped, dm_len, D2MAX)
    series = series.reshape(local_trials * DPS, dm_len)
    inside = series[:, :block_len]
    totals = lax.psum(jnp.sum(inside, axis=1), "tm")
    average = totals / total_len
    centred = lax.psum(jnp.sum((inside - average[:, None]) ** 2, axis=1), "tm")
    spread = centred / total_len
    deviation = jnp.sqrt(spread + 1e-05)
    normed = (series - average[:, None]) / deviation[:, None]
    local_peaks = peak_scores(normed, widths, block_len)
    return lax.pmax(local_peaks, "tm")

LOWS = 4
SUB_LOWS = 8


def fused_kernel(peers, block_len, data_hbm, chan_hbm, sub_hbm, width_hbm, out_ref,
                 data_ref, chan_ref, sub_ref, width_ref, load_sem, select, shifted, picks, moved, outgoing, incoming,
                 running, totals, send_sem, recv_sem):
    me = lax.axis_index("freq")
    rows = data_ref.shape[0]
    bands = rows // CPS
    own_trials = NSDM // peers
    dms = sub_ref.shape[0]
    group = bands * own_trials
    f32, bf16 = jnp.float32, jnp.bfloat16
    highs = D1MAX // LOWS + 1
    sub_highs = D2MAX // SUB_LOWS + 1
    blocks = block_len // 128

    loads = [
        pltpu.make_async_copy(source, target, load_sem.at[index])
        for index, (source, target) in enumerate((
            (chan_hbm, chan_ref), (data_hbm, data_ref), (sub_hbm, sub_ref), (width_hbm, width_ref)))
    ]
    for load in loads:
        load.start()

    barrier = pltpu.get_barrier_semaphore()

    def greet(step, carry):
        pl.semaphore_signal(barrier, inc=1, device_id={"freq": lax.rem(me + step, peers)},
                            device_id_type=pl.DeviceIdType.MESH)
        return carry

    lax.fori_loop(1, peers, greet, 0)

    def iota(shape, axis):
        return lax.broadcasted_iota(jnp.int32, shape, axis)

    def shift_rows(block, target, first, count, lows):
        lane = iota(block.shape, 1)
        for low in range(lows):
            piece = block
            if low:
                piece = jnp.where(lane < block_len - low, pltpu.roll(block, block_len - low, 1), jnp.zeros_like(block))
            target[low * count + first:low * count + first + block.shape[0], :] = piece

    def total_of(product, count, count_highs, lows):
        lane = iota((count, 128), 1)
        sums = [product[0:count, 128 * i:128 * (i + 1)] for i in range(blocks)]
        for high in range(1, count_highs):
            step = lows * high
            turned = [
                pltpu.roll(product[high * count:(high + 1) * count, 128 * i:128 * (i + 1)], 128 - step, 1)
                for i in range(blocks)
            ] + [0.0]
            for i in range(blocks):
                sums[i] = sums[i] + jnp.where(lane < 128 - step, turned[i], turned[i + 1])
        return sums

    def pick_trials(first, count):
        lane = iota((count, rows), 1)
        chan = chan_ref[first:first + count, :]
        other = pltpu.roll(chan, CPS, 1)
        for band in range(bands):
            near, far = (chan, other) if band == 0 else (other, chan)
            pair = jnp.where(lane < CPS, near, far - 1)
            for high in range(highs):
                for half in range(LOWS // 2):
                    block = jnp.where(pair == LOWS * high + 2 * half, 1.0, 0.0).astype(bf16)
                    start = highs * first + high * count
                    select[band, start:start + count, 128 * half:128 * (half + 1)] = block

    def form(first, count):
        for band in range(bands):
            start = highs * first
            product = jnp.dot(select[band, start:start + highs * count, :], shifted[band],
                              preferred_element_type=f32)
            sums = total_of(product, count, highs, LOWS)
            for i in range(blocks):
                outgoing[first // own_trials:(first + count) // own_trials, own_trials * band:own_trials * (band + 1),
                         128 * i:128 * (i + 1)] = sums[i].astype(bf16).reshape(count // own_trials, own_trials, 128)

    quarter = peers // 4

    def sending(target):
        return pltpu.make_async_remote_copy(
            src_ref=outgoing.at[target], dst_ref=incoming.at[me],
            send_sem=send_sem, recv_sem=recv_sem.at[me // quarter],
            device_id={"freq": target}, device_id_type=pl.DeviceIdType.MESH)

    def start_one(target, carry):
        @pl.when(target != me)
        def _():
            sending(target).start()
        return carry

    first_trials = NSDM // 4
    loads[0].wait()
    pick_trials(0, first_trials)
    loads[1].wait()
    for band in range(bands):
        shift_rows(data_ref[band * CPS:(band + 1) * CPS, :], shifted.at[band], 0, CPS, LOWS)
    form(0, first_trials)
    last = me >= peers - 2

    def meet():
        pl.semaphore_wait(barrier, peers - 1)
        lax.fori_loop(0, 2, start_one, 0)

    pl.when(last)(meet)
    pick_trials(first_trials, NSDM - first_trials)
    form(first_trials, NSDM - first_trials)
    pl.when(jnp.logical_not(last))(meet)

    def start_rest(step, carry):
        target = lax.rem(me + step, peers)
        @pl.when(target >= 2)
        def _():
            start_one(target, carry)
        return carry

    lax.fori_loop(0, peers, start_rest, 0)
    own = pltpu.make_async_copy(outgoing.at[me], incoming.at[me], recv_sem.at[me // quarter])
    own.start()

    loads[2].wait()
    loads[3].wait()
    trial_dms = dms // own_trials
    half_rows = rows // 2
    sub = sub_ref[...].astype(f32).astype(bf16)
    for half in range(2):
        lane = iota((NSUB, 128), 1)
        row = half * half_rows + lane % half_rows
        spread = (row // own_trials == iota((NSUB, 128), 0)).astype(f32).astype(bf16)
        delay = jnp.dot(sub, spread, preferred_element_type=f32)
        lane = iota((dms, 128), 1)
        delay = delay - (lane // half_rows).astype(f32)
        delay = jnp.where(lane % own_trials == iota((dms, 128), 0) // trial_dms, delay, -99.0)
        for high in range(sub_highs):
            for pair in range(SUB_LOWS // 2):
                picks[half, high * dms:(high + 1) * dms, 128 * pair:128 * (pair + 1)] = jnp.where(
                    delay == float(SUB_LOWS * high + 2 * pair), 1.0, 0.0).astype(bf16)
    before = jnp.where(iota((256, 256), 1) < 128, iota((256, 256), 0) % 128 - iota((256, 256), 1), -1) < 0
    totals[...] = before.astype(f32).astype(bf16)

    def arrived(index, place):
        part = incoming.at[pl.ds(index * quarter, quarter)]
        pltpu.make_async_copy(part, part, recv_sem.at[index]).wait()
        block = jnp.concatenate(
            [incoming[pl.ds(index * quarter, quarter), :, 128 * i:128 * (i + 1)].reshape(rows // 4, 128)
             for i in range(blocks)], axis=1)
        shift_rows(block, moved.at[index // 2], place * (rows // 4), half_rows, SUB_LOWS)

    def half_series(half):
        arrived(2 * half, 0)
        arrived(2 * half + 1, 1)
        return total_of(jnp.dot(picks[half], moved[half], preferred_element_type=f32), dms, sub_highs, SUB_LOWS)

    near = (2 * me) // peers
    series = [a + b for a, b in zip(half_series(near), half_series(1 - near))]
    average = jnp.sum(sum(series), axis=1, keepdims=True) / block_len
    centred = [block - average for block in series]
    spread = jnp.sum(sum(block * block for block in centred), axis=1, keepdims=True) / block_len
    deviation = jnp.sqrt(spread + 1e-05)
    across = jnp.broadcast_to(deviation, (dms, 128)).T[0:1, :]
    stacked = jnp.concatenate(centred, axis=0)
    head = stacked.astype(bf16)
    tail = (stacked - head.astype(f32)).astype(bf16)
    sums = jnp.dot(jnp.concatenate([head, tail], axis=1), totals[...], preferred_element_type=f32)
    carry = jnp.zeros((dms, 128), f32)
    pieces = []
    for i in range(blocks):
        block = sums[i * dms:(i + 1) * dms, :]
        pieces.append(block[:, 0:128] + carry)
        carry = carry + block[:, 128:256]
    for i in range(WMAX // 128):
        pieces.append(carry - average * (iota((dms, 128), 1) + 128 * i).astype(f32))
    for i in range(blocks):
        running[128 * i:128 * (i + 1), :] = jnp.concatenate([pieces[i], pieces[i + 2]], axis=0).T

    span = block_len - 256
    tile = 64
    count = width_ref.shape[0]
    widths = [width_ref[index] for index in range(count)]
    best = [None] * count
    for start in range(0, span, tile):
        base = running[start:start + tile, :]
        for index in range(count):
            rise = running[pl.ds(widths[index] + start, tile), :] - base
            rise = jnp.max(rise.reshape(tile // 8, 8, 2 * dms), axis=0)
            best[index] = rise if start == 0 else jnp.maximum(best[index], rise)
    peaks = [jnp.max(rise, axis=0, keepdims=True) for rise in best]
    peaks = jnp.concatenate(peaks, axis=0)
    peaks = jnp.maximum(peaks, pltpu.roll(peaks, dms, 1))
    scales = jnp.concatenate(
        [jnp.full((1, dms), width_ref[index].astype(f32)) for index in range(width_ref.shape[0])], axis=0)
    out_ref[...] = peaks[:, 0:dms] / (across * jnp.sqrt(scales))
    sent = outgoing.at[0:peers - 1]
    pltpu.make_async_copy(sent, sent, send_sem).wait()


def fused(data, chan_delay, sub_delay, widths):
    peers = lax.axis_size("freq")
    rows, block_len = data.shape
    bands = rows // CPS
    dms = sub_delay.shape[0]
    group = bands * (NSDM // peers)
    highs = D1MAX // LOWS + 1
    sub_highs = D2MAX // SUB_LOWS + 1
    anywhere = pl.BlockSpec(memory_space=pl.ANY)
    peaks = pl.pallas_call(
        functools.partial(fused_kernel, peers, block_len),
        out_shape=pltpu.VMEM((widths.shape[0], dms), jnp.float32),
        in_specs=[anywhere] * 4,
        out_specs=pl.BlockSpec(memory_space=pltpu.VMEM),
        scratch_shapes=[
            pltpu.VMEM(data.shape, data.dtype),
            pltpu.VMEM(chan_delay.shape, chan_delay.dtype),
            pltpu.VMEM(sub_delay.shape, sub_delay.dtype),
            pltpu.SMEM(widths.shape, widths.dtype),
            pltpu.SemaphoreType.DMA((4,)),
            pltpu.VMEM((bands, highs * NSDM, LOWS * CPS), jnp.bfloat16),
            pltpu.VMEM((bands, LOWS * CPS, block_len), jnp.bfloat16),
            pltpu.VMEM((2, sub_highs * dms, SUB_LOWS * rows // 2), jnp.bfloat16),
            pltpu.VMEM((2, SUB_LOWS * rows // 2, block_len), jnp.bfloat16),
            pltpu.VMEM((peers, group, block_len), jnp.bfloat16),
            pltpu.VMEM((peers, group, block_len), jnp.bfloat16),
            pltpu.VMEM((block_len, 2 * dms), jnp.float32),
            pltpu.VMEM((256, 256), jnp.bfloat16),
            pltpu.SemaphoreType.DMA,
            pltpu.SemaphoreType.DMA((4,)),
        ],
        compiler_params=pltpu.CompilerParams(collective_id=0, has_side_effects=True),
    )(data, chan_delay, sub_delay, widths)
    return peaks.T


def solution(mesh):
    in_specs = (P(("beam", "freq"), "tm"), P(None, "freq"), P("freq", None), P())
    out_specs = P(("beam", "freq"), None)
    whole_time = mesh.shape["tm"] == 1 and mesh.shape["freq"] % 8 == 0
    return jax.shard_map(
        fused if whole_time else on_device, mesh=mesh, in_specs=in_specs, out_specs=out_specs, check_vma=False
    )
```

```python
import functools

import jax
import jax.numpy as jnp
from jax import lax
from jax.experimental import pallas as pl
from jax.experimental.pallas import tpu as pltpu
from jax.sharding import PartitionSpec as P

NSUB = 64
NSDM = 64
WMAX = 256
CPS = 64
DPS = 32
D1MAX = 40
D2MAX = 24


def passed_along(value, axis, steps):
    count = lax.axis_size(axis)
    initial, last = (max(0, -steps), min(count, count - steps))
    return lax.ppermute(value, axis, [(source, source + steps) for source in range(initial, last)])


def shifted_sum(source, delays, length, largest):
    band_count = source.shape[0]
    trial_count = delays.shape[1]
    start_total = jnp.zeros((band_count, trial_count, length), jnp.float32)

    def add_shifts(step_index, running_total):
        for within in range(2):
            offset = 2 * step_index + within
            window = lax.dynamic_slice_in_dim(source, offset, length, 2)
            selector = (delays == offset).astype(jnp.bfloat16)
            running_total = running_total + jnp.einsum(
                "bsm,bmt->bst", selector, window, preferred_element_type=jnp.float32
            )
        return running_total

    return lax.fori_loop(0, (largest + 2) // 2, add_shifts, start_total)


def form_subbands(extended, chan_delay, length):
    band_count = extended.shape[0] // CPS
    channel_slabs = extended.reshape(band_count, CPS, extended.shape[1])
    trial_delays = chan_delay.reshape(NSDM, band_count, CPS).transpose(1, 0, 2)
    return shifted_sum(channel_slabs, trial_delays, length, D1MAX).astype(jnp.bfloat16)


def prefix_sums(values):
    step = 1
    while step < values.shape[1]:
        values = values + jnp.pad(values[:, :-step], ((0, 0), (step, 0)))
        step *= 2
    return values


def peak_scores(normed, widths, span):
    running = jnp.concatenate([jnp.zeros((normed.shape[0], 1), normed.dtype), prefix_sums(normed)], axis=1)

    def one_width(width):
        upper = lax.dynamic_slice_in_dim(running, width, span, 1)
        return jnp.max((upper - running[:, :span]) / jnp.sqrt(width.astype(jnp.float32)), axis=1)

    return lax.map(one_width, widths).T


def on_device(data, chan_delay, sub_delay, widths):
    block_len = data.shape[1]
    total_len = block_len * lax.axis_size("tm")
    edge_rows = passed_along(data[:, :D1MAX], "tm", -1)
    extended = jnp.concatenate([data, edge_rows], axis=1)
    subband = form_subbands(extended, chan_delay, block_len)
    regrouped = lax.all_to_all(subband, "freq", split_axis=1, concat_axis=0, tiled=True)
    later = passed_along(regrouped[:, :, : D2MAX + WMAX], "tm", -1)
    regrouped = jnp.concatenate([regrouped, later], axis=2)
    dm_len = block_len + WMAX
    local_trials = regrouped.shape[1]
    grouped = sub_delay.reshape(local_trials, DPS, NSUB)
    by_trial = jnp.transpose(regrouped, (1, 0, 2))
    series = shifted_sum(by_trial, grouped, dm_len, D2MAX)
    series = series.reshape(local_trials * DPS, dm_len)
    inside = series[:, :block_len]
    totals = lax.psum(jnp.sum(inside, axis=1), "tm")
    average = totals / total_len
    centred = lax.psum(jnp.sum((inside - average[:, None]) ** 2, axis=1), "tm")
    spread = centred / total_len
    deviation = jnp.sqrt(spread + 1e-05)
    normed = (series - average[:, None]) / deviation[:, None]
    local_peaks = peak_scores(normed, widths, block_len)
    return lax.pmax(local_peaks, "tm")

LOWS = 4
SUB_LOWS = 8


def fused_kernel(peers, block_len, data_hbm, chan_hbm, sub_hbm, width_hbm, out_ref,
                 data_ref, chan_ref, sub_ref, width_ref, load_sem, select, shifted, picks, moved, outgoing, incoming,
                 running, totals, send_sem, recv_sem):
    me = lax.axis_index("freq")
    rows = data_ref.shape[0]
    bands = rows // CPS
    own_trials = NSDM // peers
    dms = sub_ref.shape[0]
    group = bands * own_trials
    f32, bf16 = jnp.float32, jnp.bfloat16
    highs = D1MAX // LOWS + 1
    sub_highs = D2MAX // SUB_LOWS + 1
    blocks = block_len // 128

    loads = [
        pltpu.make_async_copy(source, target, load_sem.at[index])
        for index, (source, target) in enumerate((
            (chan_hbm, chan_ref), (data_hbm, data_ref), (sub_hbm, sub_ref), (width_hbm, width_ref)))
    ]
    for load in loads:
        load.start()

    barrier = pltpu.get_barrier_semaphore()

    def greet(step, carry):
        pl.semaphore_signal(barrier, inc=1, device_id={"freq": lax.rem(me + step, peers)},
                            device_id_type=pl.DeviceIdType.MESH)
        return carry

    lax.fori_loop(1, peers, greet, 0)

    def iota(shape, axis):
        return lax.broadcasted_iota(jnp.int32, shape, axis)

    def shift_rows(block, target, first, count, lows):
        lane = iota(block.shape, 1)
        for low in range(lows):
            piece = block
            if low:
                piece = jnp.where(lane < block_len - low, pltpu.roll(block, block_len - low, 1), jnp.zeros_like(block))
            target[low * count + first:low * count + first + block.shape[0], :] = piece

    def total_of(product, count, count_highs, lows):
        lane = iota((count, 128), 1)
        sums = [product[0:count, 128 * i:128 * (i + 1)] for i in range(blocks)]
        for high in range(1, count_highs):
            step = lows * high
            turned = [
                pltpu.roll(product[high * count:(high + 1) * count, 128 * i:128 * (i + 1)], 128 - step, 1)
                for i in range(blocks)
            ] + [0.0]
            for i in range(blocks):
                sums[i] = sums[i] + jnp.where(lane < 128 - step, turned[i], turned[i + 1])
        return sums

    def pick_trials(first, count):
        lane = iota((count, rows), 1)
        chan = chan_ref[first:first + count, :]
        other = pltpu.roll(chan, CPS, 1)
        for band in range(bands):
            near, far = (chan, other) if band == 0 else (other, chan)
            pair = jnp.where(lane < CPS, near, far - 1)
            for high in range(highs):
                for half in range(LOWS // 2):
                    block = jnp.where(pair == LOWS * high + 2 * half, 1.0, 0.0).astype(bf16)
                    start = highs * first + high * count
                    select[band, start:start + count, 128 * half:128 * (half + 1)] = block

    def form(first, count):
        for band in range(bands):
            start = highs * first
            product = jnp.dot(select[band, start:start + highs * count, :], shifted[band],
                              preferred_element_type=f32)
            sums = total_of(product, count, highs, LOWS)
            for i in range(blocks):
                outgoing[first // own_trials:(first + count) // own_trials, own_trials * band:own_trials * (band + 1),
                         128 * i:128 * (i + 1)] = sums[i].astype(bf16).reshape(count // own_trials, own_trials, 128)

    quarter = peers // 4

    def sending(target):
        return pltpu.make_async_remote_copy(
            src_ref=outgoing.at[target], dst_ref=incoming.at[me],
            send_sem=send_sem, recv_sem=recv_sem.at[me // quarter],
            device_id={"freq": target}, device_id_type=pl.DeviceIdType.MESH)

    def start_one(target, carry):
        @pl.when(target != me)
        def _():
            sending(target).start()
        return carry

    first_trials = NSDM // 4
    loads[0].wait()
    pick_trials(0, first_trials)
    loads[1].wait()
    for band in range(bands):
        shift_rows(data_ref[band * CPS:(band + 1) * CPS, :], shifted.at[band], 0, CPS, LOWS)
    form(0, first_trials)
    last = me >= peers - 2

    def meet():
        pl.semaphore_wait(barrier, peers - 1)
        lax.fori_loop(0, 2, start_one, 0)

    pl.when(last)(meet)
    pick_trials(first_trials, NSDM - first_trials)
    form(first_trials, NSDM - first_trials)
    pl.when(jnp.logical_not(last))(meet)

    def start_rest(step, carry):
        target = lax.rem(me + step, peers)
        @pl.when(target >= 2)
        def _():
            start_one(target, carry)
        return carry

    lax.fori_loop(0, peers, start_rest, 0)
    own = pltpu.make_async_copy(outgoing.at[me], incoming.at[me], recv_sem.at[me // quarter])
    own.start()

    loads[2].wait()
    loads[3].wait()
    trial_dms = dms // own_trials
    half_rows = rows // 2
    sub = sub_ref[...].astype(f32).astype(bf16)
    for half in range(2):
        lane = iota((NSUB, 128), 1)
        row = half * half_rows + lane % half_rows
        spread = (row // own_trials == iota((NSUB, 128), 0)).astype(f32).astype(bf16)
        delay = jnp.dot(sub, spread, preferred_element_type=f32)
        lane = iota((dms, 128), 1)
        delay = delay - (lane // half_rows).astype(f32)
        delay = jnp.where(lane % own_trials == iota((dms, 128), 0) // trial_dms, delay, -99.0)
        for high in range(sub_highs):
            for pair in range(SUB_LOWS // 2):
                picks[half, high * dms:(high + 1) * dms, 128 * pair:128 * (pair + 1)] = jnp.where(
                    delay == float(SUB_LOWS * high + 2 * pair), 1.0, 0.0).astype(bf16)
    before = jnp.where(iota((256, 256), 1) < 128, iota((256, 256), 0) % 128 - iota((256, 256), 1), -1) < 0
    totals[...] = before.astype(f32).astype(bf16)

    def half_series(half):
        for index in (2 * half, 2 * half + 1):
            part = incoming.at[pl.ds(index * quarter, quarter)]
            pltpu.make_async_copy(part, part, recv_sem.at[index]).wait()
        block = jnp.concatenate(
            [incoming[pl.ds(2 * half * quarter, 2 * quarter), :, 128 * i:128 * (i + 1)].reshape(half_rows, 128)
             for i in range(blocks)], axis=1)
        padded = jnp.concatenate([block, jnp.zeros((half_rows, 128), bf16)], axis=1)
        pieces = [block] + [
            pltpu.roll(padded, block_len + 128 - low, 1)[:, 0:block_len] for low in range(1, SUB_LOWS)]
        product = jnp.dot(picks[half], jnp.concatenate(pieces, axis=0), preferred_element_type=f32)
        return total_of(product, dms, sub_highs, SUB_LOWS)

    near = (2 * me) // peers
    series = [a + b for a, b in zip(half_series(near), half_series(1 - near))]
    average = jnp.sum(sum(series), axis=1, keepdims=True) / block_len
    centred = [block - average for block in series]
    spread = jnp.sum(sum(block * block for block in centred), axis=1, keepdims=True) / block_len
    deviation = jnp.sqrt(spread + 1e-05)
    across = jnp.broadcast_to(deviation, (dms, 128)).T[0:1, :]
    stacked = jnp.concatenate(centred, axis=0)
    head = stacked.astype(bf16)
    tail = (stacked - head.astype(f32)).astype(bf16)
    sums = jnp.dot(jnp.concatenate([head, tail], axis=1), totals[...], preferred_element_type=f32)
    carry = jnp.zeros((dms, 128), f32)
    pieces = []
    for i in range(blocks):
        block = sums[i * dms:(i + 1) * dms, :]
        pieces.append(block[:, 0:128] + carry)
        carry = carry + block[:, 128:256]
    for i in range(WMAX // 128):
        pieces.append(carry - average * (iota((dms, 128), 1) + 128 * i).astype(f32))
    for i in range(blocks):
        running[128 * i:128 * (i + 1), :] = jnp.concatenate([pieces[i], pieces[i + 2]], axis=0).T

    span = block_len - 256
    tile = 64
    count = width_ref.shape[0]
    widths = [width_ref[index] for index in range(count)]
    best = [None] * count
    for start in range(0, span, tile):
        base = running[start:start + tile, :]
        for index in range(count):
            rise = running[pl.ds(widths[index] + start, tile), :] - base
            rise = jnp.max(rise.reshape(tile // 8, 8, 2 * dms), axis=0)
            best[index] = rise if start == 0 else jnp.maximum(best[index], rise)
    for index in range(count):
        running[8 * index:8 * index + 8, :] = best[index]
    peaks = running[pl.ds(0, count, stride=8), :]
    for within in range(1, 8):
        peaks = jnp.maximum(peaks, running[pl.ds(within, count, stride=8), :])
    peaks = jnp.maximum(peaks, pltpu.roll(peaks, dms, 1))
    scales = jnp.concatenate(
        [jnp.full((1, dms), width_ref[index].astype(f32)) for index in range(width_ref.shape[0])], axis=0)
    out_ref[...] = peaks[:, 0:dms] / (across * jnp.sqrt(scales))
    sent = outgoing.at[0:peers - 1]
    pltpu.make_async_copy(sent, sent, send_sem).wait()


def fused(data, chan_delay, sub_delay, widths):
    peers = lax.axis_size("freq")
    rows, block_len = data.shape
    bands = rows // CPS
    dms = sub_delay.shape[0]
    group = bands * (NSDM // peers)
    highs = D1MAX // LOWS + 1
    sub_highs = D2MAX // SUB_LOWS + 1
    anywhere = pl.BlockSpec(memory_space=pl.ANY)
    peaks = pl.pallas_call(
        functools.partial(fused_kernel, peers, block_len),
        out_shape=pltpu.VMEM((widths.shape[0], dms), jnp.float32),
        in_specs=[anywhere] * 4,
        out_specs=pl.BlockSpec(memory_space=pltpu.VMEM),
        scratch_shapes=[
            pltpu.VMEM(data.shape, data.dtype),
            pltpu.VMEM(chan_delay.shape, chan_delay.dtype),
            pltpu.VMEM(sub_delay.shape, sub_delay.dtype),
            pltpu.SMEM(widths.shape, widths.dtype),
            pltpu.SemaphoreType.DMA((4,)),
            pltpu.VMEM((bands, highs * NSDM, LOWS * CPS), jnp.bfloat16),
            pltpu.VMEM((bands, LOWS * CPS, block_len), jnp.bfloat16),
            pltpu.VMEM((2, sub_highs * dms, SUB_LOWS * rows // 2), jnp.bfloat16),
            pltpu.VMEM((2, SUB_LOWS * rows // 2, block_len), jnp.bfloat16),
            pltpu.VMEM((peers, group, block_len), jnp.bfloat16),
            pltpu.VMEM((peers, group, block_len), jnp.bfloat16),
            pltpu.VMEM((block_len, 2 * dms), jnp.float32),
            pltpu.VMEM((256, 256), jnp.bfloat16),
            pltpu.SemaphoreType.DMA,
            pltpu.SemaphoreType.DMA((4,)),
        ],
        compiler_params=pltpu.CompilerParams(collective_id=0, has_side_effects=True),
    )(data, chan_delay, sub_delay, widths)
    return peaks.T


def solution(mesh):
    in_specs = (P(("beam", "freq"), "tm"), P(None, "freq"), P("freq", None), P())
    out_specs = P(("beam", "freq"), None)
    whole_time = mesh.shape["tm"] == 1 and mesh.shape["freq"] % 8 == 0
    return jax.shard_map(
        fused if whole_time else on_device, mesh=mesh, in_specs=in_specs, out_specs=out_specs, check_vma=False
    )
```

```python
import functools

import jax
import jax.numpy as jnp
from jax import lax
from jax.experimental import pallas as pl
from jax.experimental.pallas import tpu as pltpu
from jax.sharding import PartitionSpec as P

NSUB = 64
NSDM = 64
WMAX = 256
CPS = 64
DPS = 32
D1MAX = 40
D2MAX = 24


def passed_along(value, axis, steps):
    count = lax.axis_size(axis)
    initial, last = (max(0, -steps), min(count, count - steps))
    return lax.ppermute(value, axis, [(source, source + steps) for source in range(initial, last)])


def shifted_sum(source, delays, length, largest):
    band_count = source.shape[0]
    trial_count = delays.shape[1]
    start_total = jnp.zeros((band_count, trial_count, length), jnp.float32)

    def add_shifts(step_index, running_total):
        for within in range(2):
            offset = 2 * step_index + within
            window = lax.dynamic_slice_in_dim(source, offset, length, 2)
            selector = (delays == offset).astype(jnp.bfloat16)
            running_total = running_total + jnp.einsum(
                "bsm,bmt->bst", selector, window, preferred_element_type=jnp.float32
            )
        return running_total

    return lax.fori_loop(0, (largest + 2) // 2, add_shifts, start_total)


def form_subbands(extended, chan_delay, length):
    band_count = extended.shape[0] // CPS
    channel_slabs = extended.reshape(band_count, CPS, extended.shape[1])
    trial_delays = chan_delay.reshape(NSDM, band_count, CPS).transpose(1, 0, 2)
    return shifted_sum(channel_slabs, trial_delays, length, D1MAX).astype(jnp.bfloat16)


def prefix_sums(values):
    step = 1
    while step < values.shape[1]:
        values = values + jnp.pad(values[:, :-step], ((0, 0), (step, 0)))
        step *= 2
    return values


def peak_scores(normed, widths, span):
    running = jnp.concatenate([jnp.zeros((normed.shape[0], 1), normed.dtype), prefix_sums(normed)], axis=1)

    def one_width(width):
        upper = lax.dynamic_slice_in_dim(running, width, span, 1)
        return jnp.max((upper - running[:, :span]) / jnp.sqrt(width.astype(jnp.float32)), axis=1)

    return lax.map(one_width, widths).T


def on_device(data, chan_delay, sub_delay, widths):
    block_len = data.shape[1]
    total_len = block_len * lax.axis_size("tm")
    edge_rows = passed_along(data[:, :D1MAX], "tm", -1)
    extended = jnp.concatenate([data, edge_rows], axis=1)
    subband = form_subbands(extended, chan_delay, block_len)
    regrouped = lax.all_to_all(subband, "freq", split_axis=1, concat_axis=0, tiled=True)
    later = passed_along(regrouped[:, :, : D2MAX + WMAX], "tm", -1)
    regrouped = jnp.concatenate([regrouped, later], axis=2)
    dm_len = block_len + WMAX
    local_trials = regrouped.shape[1]
    grouped = sub_delay.reshape(local_trials, DPS, NSUB)
    by_trial = jnp.transpose(regrouped, (1, 0, 2))
    series = shifted_sum(by_trial, grouped, dm_len, D2MAX)
    series = series.reshape(local_trials * DPS, dm_len)
    inside = series[:, :block_len]
    totals = lax.psum(jnp.sum(inside, axis=1), "tm")
    average = totals / total_len
    centred = lax.psum(jnp.sum((inside - average[:, None]) ** 2, axis=1), "tm")
    spread = centred / total_len
    deviation = jnp.sqrt(spread + 1e-05)
    normed = (series - average[:, None]) / deviation[:, None]
    local_peaks = peak_scores(normed, widths, block_len)
    return lax.pmax(local_peaks, "tm")

LOWS = 8
SUB_LOWS = 8


def fused_kernel(peers, block_len, data_hbm, chan_hbm, sub_hbm, width_hbm, out_ref,
                 data_ref, chan_ref, sub_ref, width_ref, load_sem, select, shifted, picks, outgoing, incoming,
                 running, totals, send_sem, recv_sem):
    me = lax.axis_index("freq")
    rows = data_ref.shape[0]
    bands = rows // CPS
    own_trials = NSDM // peers
    dms = sub_ref.shape[0]
    group = bands * own_trials
    f32, bf16 = jnp.float32, jnp.bfloat16
    highs = D1MAX // LOWS + 1
    sub_highs = D2MAX // SUB_LOWS + 1
    blocks = block_len // 128

    loads = [
        pltpu.make_async_copy(source, target, load_sem.at[index])
        for index, (source, target) in enumerate((
            (chan_hbm, chan_ref), (data_hbm, data_ref), (sub_hbm, sub_ref), (width_hbm, width_ref)))
    ]
    for load in loads:
        load.start()

    barrier = pltpu.get_barrier_semaphore()

    def greet(step, carry):
        pl.semaphore_signal(barrier, inc=1, device_id={"freq": lax.rem(me + step, peers)},
                            device_id_type=pl.DeviceIdType.MESH)
        return carry

    lax.fori_loop(1, peers, greet, 0)

    def iota(shape, axis):
        return lax.broadcasted_iota(jnp.int32, shape, axis)

    def shift_rows(block, target, first, count, lows):
        padded = jnp.concatenate([block, jnp.zeros((block.shape[0], 128), block.dtype)], axis=1)
        for low in range(lows):
            piece = pltpu.roll(padded, block_len + 128 - low, 1)[:, 0:block_len] if low else block
            target[low * count + first:low * count + first + block.shape[0], :] = piece

    def total_of(product, count, count_highs, lows):
        lane = iota((count, 128), 1)
        sums = [product[0:count, 128 * i:128 * (i + 1)] for i in range(blocks)]
        for high in range(1, count_highs):
            step = lows * high
            turned = [
                pltpu.roll(product[high * count:(high + 1) * count, 128 * i:128 * (i + 1)], 128 - step, 1)
                for i in range(blocks)
            ] + [0.0]
            for i in range(blocks):
                sums[i] = sums[i] + jnp.where(lane < 128 - step, turned[i], turned[i + 1])
        return sums

    def pick_trials(first, count):
        lane = iota((count, rows), 1)
        chan = chan_ref[first:first + count, :]
        other = pltpu.roll(chan, CPS, 1)
        for band in range(bands):
            near, far = (chan, other) if band == 0 else (other, chan)
            pair = jnp.where(lane < CPS, near, far - 1)
            for high in range(highs):
                for half in range(LOWS // 2):
                    block = jnp.where(pair == LOWS * high + 2 * half, 1.0, 0.0).astype(bf16)
                    start = highs * first + high * count
                    select[band, start:start + count, 128 * half:128 * (half + 1)] = block

    def form(first, count):
        for band in range(bands):
            start = highs * first
            product = jnp.dot(select[band, start:start + highs * count, :], shifted[band],
                              preferred_element_type=f32)
            sums = total_of(product, count, highs, LOWS)
            for i in range(blocks):
                outgoing[first // own_trials:(first + count) // own_trials, own_trials * band:own_trials * (band + 1),
                         128 * i:128 * (i + 1)] = sums[i].astype(bf16).reshape(count // own_trials, own_trials, 128)

    quarter = peers // 4

    def sending(target):
        return pltpu.make_async_remote_copy(
            src_ref=outgoing.at[target], dst_ref=incoming.at[me],
            send_sem=send_sem, recv_sem=recv_sem.at[me // quarter],
            device_id={"freq": target}, device_id_type=pl.DeviceIdType.MESH)

    def start_one(target, carry):
        @pl.when(target != me)
        def _():
            sending(target).start()
        return carry

    first_trials = NSDM // 4
    loads[0].wait()
    pick_trials(0, first_trials)
    loads[1].wait()
    for band in range(bands):
        shift_rows(data_ref[band * CPS:(band + 1) * CPS, :], shifted.at[band], 0, CPS, LOWS)
    form(0, first_trials)
    last = me >= peers - 2

    def meet():
        pl.semaphore_wait(barrier, peers - 1)
        lax.fori_loop(0, 2, start_one, 0)

    pl.when(last)(meet)
    pick_trials(first_trials, NSDM - first_trials)
    form(first_trials, NSDM - first_trials)
    pl.when(jnp.logical_not(last))(meet)

    def start_rest(step, carry):
        target = lax.rem(me + step, peers)
        @pl.when(target >= 2)
        def _():
            start_one(target, carry)
        return carry

    lax.fori_loop(0, peers, start_rest, 0)
    own = pltpu.make_async_copy(outgoing.at[me], incoming.at[me], recv_sem.at[me // quarter])
    own.start()

    loads[2].wait()
    loads[3].wait()
    trial_dms = dms // own_trials
    half_rows = rows // 2
    sub = sub_ref[...].astype(f32).astype(bf16)
    for half in range(2):
        lane = iota((NSUB, 128), 1)
        row = half * half_rows + lane % half_rows
        spread = (row // own_trials == iota((NSUB, 128), 0)).astype(f32).astype(bf16)
        delay = jnp.dot(sub, spread, preferred_element_type=f32)
        lane = iota((dms, 128), 1)
        delay = delay - (lane // half_rows).astype(f32)
        delay = jnp.where(lane % own_trials == iota((dms, 128), 0) // trial_dms, delay, -99.0)
        for high in range(sub_highs):
            for pair in range(SUB_LOWS // 2):
                picks[half, high * dms:(high + 1) * dms, 128 * pair:128 * (pair + 1)] = jnp.where(
                    delay == float(SUB_LOWS * high + 2 * pair), 1.0, 0.0).astype(bf16)
    before = jnp.where(iota((256, 256), 1) < 128, iota((256, 256), 0) % 128 - iota((256, 256), 1), -1) < 0
    totals[...] = before.astype(f32).astype(bf16)

    def half_series(half):
        for index in (2 * half, 2 * half + 1):
            part = incoming.at[pl.ds(index * quarter, quarter)]
            pltpu.make_async_copy(part, part, recv_sem.at[index]).wait()
        block = jnp.concatenate(
            [incoming[pl.ds(2 * half * quarter, 2 * quarter), :, 128 * i:128 * (i + 1)].reshape(half_rows, 128)
             for i in range(blocks)], axis=1)
        padded = jnp.concatenate([block, jnp.zeros((half_rows, 128), bf16)], axis=1)
        pieces = [block] + [
            pltpu.roll(padded, block_len + 128 - low, 1)[:, 0:block_len] for low in range(1, SUB_LOWS)]
        product = jnp.dot(picks[half], jnp.concatenate(pieces, axis=0), preferred_element_type=f32)
        return total_of(product, dms, sub_highs, SUB_LOWS)

    near = (2 * me) // peers
    series = [a + b for a, b in zip(half_series(near), half_series(1 - near))]
    average = jnp.sum(sum(series), axis=1, keepdims=True) / block_len
    centred = [block - average for block in series]
    spread = jnp.sum(sum(block * block for block in centred), axis=1, keepdims=True) / block_len
    deviation = jnp.sqrt(spread + 1e-05)
    across = jnp.broadcast_to(deviation, (dms, 128)).T[0:1, :]
    stacked = jnp.concatenate(centred, axis=0)
    head = stacked.astype(bf16)
    tail = (stacked - head.astype(f32)).astype(bf16)
    sums = jnp.dot(jnp.concatenate([head, tail], axis=1), totals[...], preferred_element_type=f32)
    carry = jnp.zeros((dms, 128), f32)
    pieces = []
    for i in range(blocks):
        block = sums[i * dms:(i + 1) * dms, :]
        pieces.append(block[:, 0:128] + carry)
        carry = carry + block[:, 128:256]
    for i in range(WMAX // 128):
        pieces.append(carry - average * (iota((dms, 128), 1) + 128 * i).astype(f32))
    for i in range(blocks):
        running[128 * i:128 * (i + 1), :] = jnp.concatenate([pieces[i], pieces[i + 2]], axis=0).T

    span = block_len - 256
    tile = 64
    count = width_ref.shape[0]
    widths = [width_ref[index] for index in range(count)]
    best = [None] * count
    for start in range(0, span, tile):
        base = running[start:start + tile, :]
        for index in range(count):
            rise = running[pl.ds(widths[index] + start, tile), :] - base
            rise = jnp.max(rise.reshape(tile // 8, 8, 2 * dms), axis=0)
            best[index] = rise if start == 0 else jnp.maximum(best[index], rise)
    for index in range(count):
        running[8 * index:8 * index + 8, :] = best[index]
    peaks = running[pl.ds(0, count, stride=8), :]
    for within in range(1, 8):
        peaks = jnp.maximum(peaks, running[pl.ds(within, count, stride=8), :])
    peaks = jnp.maximum(peaks, pltpu.roll(peaks, dms, 1))
    scales = jnp.concatenate(
        [jnp.full((1, dms), width_ref[index].astype(f32)) for index in range(width_ref.shape[0])], axis=0)
    out_ref[...] = peaks[:, 0:dms] / (across * jnp.sqrt(scales))
    sent = outgoing.at[0:peers - 1]
    pltpu.make_async_copy(sent, sent, send_sem).wait()


def fused(data, chan_delay, sub_delay, widths):
    peers = lax.axis_size("freq")
    rows, block_len = data.shape
    bands = rows // CPS
    dms = sub_delay.shape[0]
    group = bands * (NSDM // peers)
    highs = D1MAX // LOWS + 1
    sub_highs = D2MAX // SUB_LOWS + 1
    anywhere = pl.BlockSpec(memory_space=pl.ANY)
    peaks = pl.pallas_call(
        functools.partial(fused_kernel, peers, block_len),
        out_shape=pltpu.VMEM((widths.shape[0], dms), jnp.float32),
        in_specs=[anywhere] * 4,
        out_specs=pl.BlockSpec(memory_space=pltpu.VMEM),
        scratch_shapes=[
            pltpu.VMEM(data.shape, data.dtype),
            pltpu.VMEM(chan_delay.shape, chan_delay.dtype),
            pltpu.VMEM(sub_delay.shape, sub_delay.dtype),
            pltpu.SMEM(widths.shape, widths.dtype),
            pltpu.SemaphoreType.DMA((4,)),
            pltpu.VMEM((bands, highs * NSDM, LOWS * CPS), jnp.bfloat16),
            pltpu.VMEM((bands, LOWS * CPS, block_len), jnp.bfloat16),
            pltpu.VMEM((2, sub_highs * dms, SUB_LOWS * rows // 2), jnp.bfloat16),
            pltpu.VMEM((peers, group, block_len), jnp.bfloat16),
            pltpu.VMEM((peers, group, block_len), jnp.bfloat16),
            pltpu.VMEM((block_len, 2 * dms), jnp.float32),
            pltpu.VMEM((256, 256), jnp.bfloat16),
            pltpu.SemaphoreType.DMA,
            pltpu.SemaphoreType.DMA((4,)),
        ],
        compiler_params=pltpu.CompilerParams(collective_id=0, has_side_effects=True),
    )(data, chan_delay, sub_delay, widths)
    return peaks.T


def solution(mesh):
    in_specs = (P(("beam", "freq"), "tm"), P(None, "freq"), P("freq", None), P())
    out_specs = P(("beam", "freq"), None)
    whole_time = mesh.shape["tm"] == 1 and mesh.shape["freq"] % 8 == 0
    return jax.shard_map(
        fused if whole_time else on_device, mesh=mesh, in_specs=in_specs, out_specs=out_specs, check_vma=False
    )
```
